32 devices in a mesh: grp: 2 (over y), seq: 4 (over z), head: 4 (over x, core).
Axes of the slice: x: 2, y: 2, z: 4, core: 2. Of those that a mesh axis runs over, the one named last changes fastest.
Arguments:
- lin_q: bfloat16 [1024, 2048], P(('grp', 'seq'), 'head'), parts along dimension 0, may hold values from -6 to 6
- lin_k: bfloat16 [1024, 2048], P(('grp', 'seq'), 'head'), parts along dimension 0, may hold values from -6 to 6
- lin_v: bfloat16 [1024, 4096], P(('grp', 'seq'), 'head'), parts along dimension 0, may hold values from -6 to 6
- conv_q: bfloat16 [4, 2048], P(None, 'head'), may hold values from -3 to 3
- conv_k: bfloat16 [4, 2048], P(None, 'head'), may hold values from -3 to 3
- conv_v: bfloat16 [4, 4096], P(None, 'head'), may hold values from -3 to 3
- lin_z: bfloat16 [1024, 4096], P(('grp', 'seq'), 'head'), parts along dimension 0, may hold values from -6 to 6
- beta_logit: float32 [1024, 32], P(('grp', 'seq'), 'head'), parts along dimension 0, may hold values from -7 to 2
- log_decay: float32 [1024, 32], P(('grp', 'seq'), 'head'), parts along dimension 0, may hold values from -1.1 to 0
- attn_query: bfloat16 [1024, 4096], P(('grp', 'seq'), 'head'), parts along dimension 0, may hold values from -6 to 6
- attn_gate: bfloat16 [1024, 4096], P(('grp', 'seq'), 'head'), parts along dimension 0, may hold values from -6 to 6
- attn_kv: bfloat16 [1024, 2, 2, 256], P(('grp', 'seq')), parts along dimension 0, may hold values from -6 to 6
- doc_lengths: int32 [10], P('grp'), parts along dimension 0, may hold values from 1 to 128, 512 in all
Outputs:
- delta_out: bfloat16 [1024, 4096], P(('grp', 'seq'), 'head'), parts along dimension 0
- attn_out: bfloat16 [1024, 4096], P(('grp', 'seq'), 'head'), parts along dimension 0
The draws below stay inside these ranges and needn't reach their ends.
There are 2 independent parts, one for each index of `grp`. The reference program is written for one: setup_inputs(seed, part) draws one part's arguments, and reference() takes and returns one part's arrays. A program takes and returns all parts, laid end to end along the dimension named above; an argument that names none is the same for every part. Nothing has to cross between parts.
Inputs may be any that keep to these rules, and one draw needn't show every extreme that they name: `doc_lengths`: the 5 documents packed in order into the slab; their lengths sum to 512.
All inputs are finite; a program needn't handle non-finite values.
Results may differ from the reference program's by a relative error of at most 0.0037.
Values may be sent and summed in bfloat16 or wider, within the bound.
A program may use at most 192 MiB of HBM per device.

```python
import math
import jax
import jax.numpy as jnp
import numpy as np
from jax import lax

DK = 128
DV = 128
QKH = 16
VALUE_HEADS = 32
CONV = 4
AQ = 16
KVH = 2
AD = 256
DOCS = 5
TOK_DEV = 128
SLAB_TOKENS = 512


def head_pace(key):
    chance = 0.5
    return jax.random.bernoulli(jax.random.fold_in(key, 11), chance, (VALUE_HEADS,))


def log_range(key, shape, lowest, highest):
    return jnp.exp(jax.random.uniform(key, shape, jnp.float32, math.log(lowest), math.log(highest)))


def draw_log_decay(key, part):
    slow_heads = head_pace(key)
    random_key_split = jax.random.split(jax.random.fold_in(key, 23), 6)
    fast_rate = log_range(random_key_split[0], (VALUE_HEADS,), 0.03, 0.1)
    slow_rate = log_range(random_key_split[1], (VALUE_HEADS,), 0.05, 0.3) / SLAB_TOKENS
    head_decay_rate = jnp.where(slow_heads, slow_rate, fast_rate)
    block_count = SLAB_TOKENS // TOK_DEV
    block_multiplier = jnp.repeat(log_range(random_key_split[2], (block_count, VALUE_HEADS), 0.5, 2.0), TOK_DEV, axis=0)
    token_multiplier = log_range(random_key_split[3], (SLAB_TOKENS, VALUE_HEADS), 0.5, 2.0)
    group_rows = jax.random.randint(random_key_split[4], (2,), 0, SLAB_TOKENS)
    group_length = jax.random.uniform(random_key_split[5], (2, VALUE_HEADS), jnp.float32, 0.22, 0.69)
    matched_rows = (jnp.arange(SLAB_TOKENS)[:, None] == group_rows[None, :]).astype(jnp.float32)
    row_groups = jnp.sum(matched_rows[:, :, None] * group_length[None, :, :], axis=1)
    return -(head_decay_rate[None, :] * block_multiplier * token_multiplier) - row_groups


def draw_beta_logit(key, part):
    slow_heads = head_pace(key)
    lowest = jnp.where(slow_heads, -7.0, -2.5)
    highest = jnp.where(slow_heads, -4.5, 2.0)
    fraction = jax.random.uniform(jax.random.fold_in(key, 31), (SLAB_TOKENS, VALUE_HEADS), jnp.float32)
    return lowest[None, :] + (highest - lowest)[None, :] * fraction


def draw_attn_query(key, part):
    base_key = jax.random.fold_in(key, 43)
    drawn = jnp.clip(jax.random.normal(base_key, (SLAB_TOKENS, AQ * AD), jnp.float32), -6.0, 6.0)
    return drawn.astype(jnp.bfloat16)


def draw_attn_kv(key, part):
    base_key = jax.random.fold_in(key, 53)
    drawn = jnp.clip(jax.random.normal(base_key, (SLAB_TOKENS, 2, KVH, AD), jnp.float32), -6.0, 6.0)
    return drawn.astype(jnp.bfloat16)


def block_scale(key, shape, pieces, least, top_value):
    def one(axis_at, blocks):
        steps = jax.random.uniform(jax.random.fold_in(jax.random.fold_in(key, 6), axis_at), (blocks,), jnp.float32, least / len(pieces), top_value / len(pieces))
        return jnp.repeat(jnp.exp(steps), shape[axis_at] // blocks).reshape((-1,) + (1,) * (len(shape) - axis_at - 1))

    loudness = one(*pieces[0])
    for cut in pieces[1:]:
        loudness = loudness * one(*cut)
    return loudness


def profile(amount, total, reach, lean):
    loads = [(1 << 20) // math.isqrt(grade ** lean) + 1 for grade in range(2, amount + 1)]
    rest, holding = total - reach - (amount - 1), [1] * (amount - 1)
    while rest > 0:
        candidates = [i for i in range(amount - 1) if holding[i] < reach]
        pool, remaining = sum([loads[i] for i in candidates]), rest
        for i in candidates:
            extra = min(reach - holding[i], max(1, remaining * loads[i] // pool), rest)
            holding[i] = holding[i] + extra
            rest = rest - extra
    return np.array([reach] + holding)


def ragged_sizes(key, count, total, limit, skew):
    if count == 2:
        one = jax.random.randint(key, (), max(1, total - limit), min(limit, total - 1) + 1)
        return jnp.stack([one, total - one])
    sizes = jnp.asarray(profile(count, total, limit, skew), jnp.int32)
    couples = (count - 1) // 2
    source_of, receiver = sizes[1:1 + 2 * couples:2], sizes[2:2 + 2 * couples:2]
    room = jnp.minimum(source_of - 1, limit - receiver)
    shifted = jax.random.randint(jax.random.fold_in(key, 1), (couples,), 0, 1 << 20) % (room + 1)
    sizes = sizes.at[1:1 + 2 * couples:2].set(source_of - shifted).at[2:2 + 2 * couples:2].set(receiver + shifted)
    return sizes[jax.random.permutation(jax.random.fold_in(key, 2), count)]


def gaussian(rng, dims, width, limit, shards=(), kind=jnp.bfloat16):
    loudness = block_scale(rng, dims, shards, -0.22, 0.18) if shards else 1.0
    entries = jax.random.normal(rng, dims, jnp.float32) * width * loudness
    return jnp.minimum(jnp.maximum(entries, -limit), limit).astype(kind)


def setup_inputs(seed: int = 0, part: int = 0) -> dict:
    arg_keys = jax.random.split(jax.random.key(seed), 14)
    own_keys = jax.random.split(jax.random.fold_in(arg_keys[13], part), 14)
    lin_q = gaussian(own_keys[0], (SLAB_TOKENS, QKH * DK), 1.0, 6.0, ((0, 4), (1, 4)))
    lin_k = gaussian(own_keys[1], (SLAB_TOKENS, QKH * DK), 1.0, 6.0, ((0, 4), (1, 4)))
    lin_v = gaussian(own_keys[2], (SLAB_TOKENS, VALUE_HEADS * DV), 1.0, 6.0, ((0, 4), (1, 4)))
    conv_q = gaussian(arg_keys[3], (CONV, QKH * DK), CONV ** -0.5, 3.0, ((1, 4),))
    conv_k = gaussian(arg_keys[4], (CONV, QKH * DK), CONV ** -0.5, 3.0, ((1, 4),))
    conv_v = gaussian(arg_keys[5], (CONV, VALUE_HEADS * DV), CONV ** -0.5, 3.0, ((1, 4),))
    lin_z = gaussian(own_keys[6], (SLAB_TOKENS, VALUE_HEADS * DV), 1.0, 6.0, ((0, 4), (1, 4)))
    beta_logit = draw_beta_logit(jax.random.fold_in(jax.random.fold_in(arg_keys[13], part), 71), part)
    log_decay = draw_log_decay(jax.random.fold_in(jax.random.fold_in(arg_keys[13], part), 71), part)
    attn_query = draw_attn_query(jax.random.fold_in(jax.random.fold_in(arg_keys[13], part), 71), part)
    attn_gate = gaussian(own_keys[10], (SLAB_TOKENS, AQ * AD), 1.0, 6.0, ((0, 4), (1, 4)))
    attn_kv = draw_attn_kv(jax.random.fold_in(jax.random.fold_in(arg_keys[13], part), 71), part)
    doc_lengths = ragged_sizes(own_keys[12], DOCS, SLAB_TOKENS, SLAB_TOKENS // 4, 0).astype(jnp.int32)
    return {"lin_q": lin_q, "lin_k": lin_k, "lin_v": lin_v, "conv_q": conv_q, "conv_k": conv_k, "conv_v": conv_v, "lin_z": lin_z, "beta_logit": beta_logit, "log_decay": log_decay, "attn_query": attn_query, "attn_gate": attn_gate, "attn_kv": attn_kv, "doc_lengths": doc_lengths}


EXACT_PRECISION = lax.Precision.HIGHEST
NEGATIVE = -1e+30

def segment_ids(positions, doc_lengths):
    offsets = jnp.cumsum(doc_lengths) - doc_lengths
    return lax.optimization_barrier(jnp.sum((offsets[None, :] <= positions[:, None]).astype(jnp.int32), axis=1))

def start_flags(positions, doc_lengths):
    offsets = jnp.cumsum(doc_lengths) - doc_lengths
    return jnp.any(offsets[None, :] == positions[:, None], axis=1)

def causal_conv(values, weights, positions, segment, doc_lengths):
    row_count = values.shape[0]
    tap_count = weights.shape[0]
    padding = jnp.zeros((tap_count - 1, values.shape[1]), jnp.float32)
    extended = jnp.concatenate([padding, values.astype(jnp.float32)], axis=0)
    conv_sum = jnp.zeros(values.shape, jnp.float32)
    for tap_index in range(tap_count):
        source = positions - (tap_count - 1) + tap_index
        inside = (segment_ids(source, doc_lengths) == segment).astype(jnp.float32)
        conv_sum = conv_sum + extended[tap_index:tap_index + row_count] * weights[tap_index].astype(jnp.float32)[None, :] * inside[:, None]
    return jax.nn.silu(conv_sum)

def unit_heads(values, head_size):
    shaped = values.reshape(values.shape[0], -1, head_size)
    return shaped * lax.rsqrt(lax.optimization_barrier(jnp.sum(shaped * shaped, axis=-1, keepdims=True)) + 1e-06)

def reference(lin_q, lin_k, lin_v, conv_q, conv_k, conv_v, lin_z, beta_logit, log_decay, attn_query, attn_gate, attn_kv, doc_lengths):
    positions = jnp.arange(SLAB_TOKENS, dtype=jnp.int32)
    segment = segment_ids(positions, doc_lengths)
    starts = start_flags(positions, doc_lengths)
    queries = unit_heads(causal_conv(lin_q, conv_q, positions, segment, doc_lengths), DK) * DK ** (-0.5)
    keys_unit = unit_heads(causal_conv(lin_k, conv_k, positions, segment, doc_lengths), DK)
    values = causal_conv(lin_v, conv_v, positions, segment, doc_lengths).reshape(SLAB_TOKENS, VALUE_HEADS, DV)
    queries = jnp.repeat(queries, VALUE_HEADS // QKH, axis=1)
    keys_unit = jnp.repeat(keys_unit, VALUE_HEADS // QKH, axis=1)
    beta_gate = jax.nn.sigmoid(beta_logit)
    decay_rates = jnp.exp(log_decay) * (1.0 - starts.astype(jnp.float32))[:, None]

    def advance(recurrent_state, inputs):
        query_transposed, key_transposed, value_t, beta_t, rate_t = inputs
        projected_input = jnp.einsum('bg,bgm->bm', key_transposed, recurrent_state, precision=EXACT_PRECISION)
        recurrent_state = rate_t[:, None, None] * (recurrent_state - beta_t[:, None, None] * key_transposed[:, :, None] * projected_input[:, None, :]) + beta_t[:, None, None] * key_transposed[:, :, None] * value_t[:, None, :]
        return (recurrent_state, jnp.einsum('bg,bgm->bm', query_transposed, recurrent_state, precision=EXACT_PRECISION))
    _, delta_output = lax.scan(advance, jnp.zeros((VALUE_HEADS, DK, DV), jnp.float32), (queries, keys_unit, values, beta_gate, decay_rates))
    inverse_rms = lax.rsqrt(lax.optimization_barrier(jnp.mean(delta_output * delta_output, axis=-1, keepdims=True)) + 1e-06)
    gate_z = jax.nn.silu(lin_z.astype(jnp.float32).reshape(SLAB_TOKENS, VALUE_HEADS, DV))
    delta_out = (delta_output * inverse_rms * gate_z).astype(jnp.bfloat16).reshape(SLAB_TOKENS, VALUE_HEADS * DV)
    query_all = attn_query.reshape(SLAB_TOKENS, KVH, AQ // KVH, AD).astype(jnp.float32)
    key_all = attn_kv[:, 0].astype(jnp.float32)
    value_all = attn_kv[:, 1].astype(jnp.float32)
    span_rows = math.gcd(SLAB_TOKENS, 256)

    def one_span(span_index):
        first_row = (span_index * span_rows).astype(jnp.int32)
        query_part = lax.dynamic_slice_in_dim(query_all, first_row, span_rows, 0)
        query_pos = first_row + jnp.arange(span_rows, dtype=jnp.int32)
        query_seg = lax.dynamic_slice_in_dim(segment, first_row, span_rows, 0)
        allowed = (positions[None, :] <= query_pos[:, None]) & (segment[None, :] == query_seg[:, None])
        scores = jnp.einsum('qcgd,kcd->cgqk', query_part, key_all, precision=EXACT_PRECISION) * AD ** (-0.5)
        masked = jnp.where(allowed, scores, NEGATIVE)
        row_top = lax.optimization_barrier(jnp.max(masked, axis=-1, keepdims=True))
        weights_f = jnp.where(allowed, jnp.exp(masked - row_top), 0.0)
        row_total = lax.optimization_barrier(jnp.sum(weights_f, axis=-1))
        rounded = lax.optimization_barrier(weights_f.astype(jnp.bfloat16)).astype(jnp.float32)
        mixture = jnp.einsum('cgqk,kcd->qcgd', rounded, value_all, precision=EXACT_PRECISION)
        mixture = mixture / jnp.transpose(row_total, (2, 0, 1))[..., None]
        return mixture.reshape(span_rows, AQ * AD)
    attended = lax.map(one_span, jnp.arange(SLAB_TOKENS // span_rows, dtype=jnp.int32)).reshape(SLAB_TOKENS, AQ * AD)
    attn_out = (attended * jax.nn.sigmoid(attn_gate.astype(jnp.float32))).astype(jnp.bfloat16)
    return (delta_out, attn_out)
```

```python
import functools

import jax
import jax.numpy as jnp
from jax import lax
from jax.experimental import pallas as pl
from jax.experimental.pallas import tpu as pltpu
from jax.sharding import PartitionSpec as P

DK = 128
DV = 128
QKH = 16
VALUE_HEADS = 32
AQ = 16
KVH = 2
AD = 256
BLOCK = 64


EXACT_PRECISION = lax.Precision.HIGHEST
NEGATIVE = -1e30


def passed_along(value, axis, steps):
    count = lax.axis_size(axis)
    initial, last = (max(0, -steps), min(count, count - steps))
    return lax.ppermute(value, axis, [(source, source + steps) for source in range(initial, last)])


def prefix_2(value, axis, combine, identity):
    length, index = (lax.axis_size(axis), lax.axis_index(axis))
    everything = jax.tree.map(
        lambda part, kind: lax.all_gather(part.astype(kind), axis),
        value,
        (jnp.bfloat16, jnp.bfloat16),
    )
    start = jax.tree.map(
        lambda part, zero: jnp.broadcast_to(jnp.asarray(zero, part.dtype), part.shape),
        value,
        identity,
    )

    def step(k, before):
        reached = k < index
        new = combine(
            before, jax.tree.map(lambda part, own: part[k].astype(own.dtype), everything, value)
        )
        return jax.tree.map(lambda a, b: jnp.where(reached, a, b), new, before)

    return lax.fori_loop(0, length, step, start)


def running_sum(values):
    count = values.shape[-1]
    later = lax.broadcasted_iota(jnp.int32, (count, count), 0)
    earlier = lax.broadcasted_iota(jnp.int32, (count, count), 1)
    kept = jnp.where(later >= earlier, values[..., None, :], jnp.zeros((), values.dtype))
    return jnp.sum(kept, axis=-1)


def segment_ids(positions, doc_lengths):
    offsets = running_sum(doc_lengths) - doc_lengths
    return jnp.sum((offsets[None, :] <= positions[:, None]).astype(jnp.int32), axis=1)


def start_flags(positions, doc_lengths):
    offsets = running_sum(doc_lengths) - doc_lengths
    return jnp.any(offsets[None, :] == positions[:, None], axis=1)


def causal_conv(values, margin, weights, positions, segment, doc_lengths):
    row_count = values.shape[0]
    tap_count = weights.shape[0]
    extended = jnp.concatenate([margin, values], axis=0).astype(jnp.float32)
    conv_sum = jnp.zeros(values.shape, jnp.float32)
    for tap_index in range(tap_count):
        source = positions - (tap_count - 1) + tap_index
        inside = (segment_ids(source, doc_lengths) == segment).astype(jnp.float32)
        conv_sum = (
            conv_sum
            + extended[tap_index : tap_index + row_count]
            * weights[tap_index].astype(jnp.float32)[None, :]
            * inside[:, None]
        )
    return jax.nn.silu(conv_sum)


def unit_heads(values, head_size):
    shaped = values.reshape(values.shape[0], -1, head_size)
    return shaped * lax.rsqrt(jnp.sum(shaped * shaped, axis=-1, keepdims=True) + 1e-06)


def compose(first_pair, second_pair):
    joined_map = jnp.einsum(
        "hij,hjk->hik", second_pair[0], first_pair[0], precision=EXACT_PRECISION
    )
    joined_shift = (
        jnp.einsum("hij,hjk->hik", second_pair[0], first_pair[1], precision=EXACT_PRECISION)
        + second_pair[1]
    )
    return (joined_map, joined_shift)


def unit_lower_inverse(lower_part, block_len):
    identity = jnp.eye(block_len, dtype=jnp.float32)
    power = -lower_part
    inverse = identity + power
    for _ in range(max(block_len - 1, 1).bit_length() - 1):
        power = jnp.einsum("nhij,nhjk->nhik", power, power, precision=EXACT_PRECISION)
        inverse = jnp.einsum(
            "nhij,nhjk->nhik", inverse, identity + power, precision=EXACT_PRECISION
        )
    return inverse


def delta_blocks(queries, keys_unit, values, beta_gate, log_rates, segment, starts):
    row_count, head_count, key_size = keys_unit.shape
    value_size = values.shape[2]
    block_len = BLOCK
    block_count = row_count // block_len

    def to_blocks(array):
        return jnp.swapaxes(array.reshape((block_count, block_len) + array.shape[1:]), 1, 2)

    query_blk = to_blocks(queries)
    key_blk = to_blocks(keys_unit)
    value_blk = to_blocks(values)
    beta_blk = to_blocks(beta_gate)
    cumulative = running_sum(to_blocks(log_rates))
    segment_blk = segment.reshape(block_count, block_len)
    fresh_count = running_sum(starts.reshape(block_count, block_len).astype(jnp.int32))
    later_row = lax.broadcasted_iota(jnp.int32, (block_len, block_len), 0)
    earlier_col = lax.broadcasted_iota(jnp.int32, (block_len, block_len), 1)
    visible = (later_row >= earlier_col)[None] & (
        segment_blk[:, :, None] == segment_blk[:, None, :]
    )
    visible = visible[:, None]
    spread = cumulative[..., :, None] - cumulative[..., None, :]
    decay_mat = jnp.where(visible, jnp.exp(jnp.where(visible, spread, 0.0)), 0.0)
    carried = jnp.where((fresh_count == 0)[:, None, :], jnp.exp(cumulative), 0.0)
    key_key = jnp.einsum("nhik,nhjk->nhij", key_blk, key_blk, precision=EXACT_PRECISION)
    strict = (later_row > earlier_col).astype(jnp.float32)
    lower_part = decay_mat * strict * key_key * beta_blk[..., None, :]
    inverse = unit_lower_inverse(lower_part, block_len)
    right_side = jnp.concatenate([value_blk, carried[..., None] * key_blk], axis=-1)
    solved = jnp.einsum("nhij,nhjc->nhic", inverse, right_side, precision=EXACT_PRECISION)
    moved_values = solved[..., :value_size]
    moved_keys = solved[..., value_size:]
    query_key = jnp.einsum("nhik,nhjk->nhij", query_blk, key_blk, precision=EXACT_PRECISION)
    attend = decay_mat * query_key * beta_blk[..., None, :]
    out_zero = jnp.einsum("nhij,nhjv->nhiv", attend, moved_values, precision=EXACT_PRECISION)
    reach_part = carried[..., None] * query_blk - jnp.einsum(
        "nhij,nhjk->nhik", attend, moved_keys, precision=EXACT_PRECISION
    )
    weighted = (beta_blk * decay_mat[..., block_len - 1, :])[..., None] * key_blk
    block_map = carried[..., block_len - 1][..., None, None] * jnp.eye(
        key_size, dtype=jnp.float32
    ) - jnp.einsum("nhjk,nhjl->nhkl", weighted, moved_keys, precision=EXACT_PRECISION)
    block_shift = jnp.einsum("nhjk,nhjv->nhkv", weighted, moved_values, precision=EXACT_PRECISION)

    def advance(prefix, current):
        return (compose(prefix, current), prefix)

    eye_heads = jnp.broadcast_to(
        jnp.eye(key_size, dtype=jnp.float32), (head_count, key_size, key_size)
    )
    zero_heads = jnp.zeros((head_count, key_size, value_size), jnp.float32)
    device_pair, prefixes = lax.scan(advance, (eye_heads, zero_heads), (block_map, block_shift))
    baseline_output = out_zero + jnp.einsum(
        "nhik,nhkv->nhiv", reach_part, prefixes[1], precision=EXACT_PRECISION
    )
    complete_reach = jnp.einsum(
        "nhik,nhkl->nhil", reach_part, prefixes[0], precision=EXACT_PRECISION
    )
    return (device_pair, baseline_output, complete_reach, eye_heads, zero_heads)


def shards(
    lin_q,
    lin_k,
    lin_v,
    conv_q,
    conv_k,
    conv_v,
    lin_z,
    beta_logit,
    log_decay,
    attn_query,
    attn_gate,
    attn_kv,
    doc_lengths,
):
    row_count = lin_q.shape[0]
    seq_index = lax.axis_index("seq")
    positions = seq_index * row_count + jnp.arange(row_count, dtype=jnp.int32)
    segment = segment_ids(positions, doc_lengths)
    starts = start_flags(positions, doc_lengths)
    rim_from = row_count - conv_q.shape[0] + 1
    rim_q, rim_k, rim_v = passed_along(
        (lin_q[rim_from:], lin_k[rim_from:], lin_v[rim_from:]), "seq", 1
    )
    queries = unit_heads(
        causal_conv(lin_q, rim_q, conv_q, positions, segment, doc_lengths), DK
    ) * DK ** (-0.5)
    keys_unit = unit_heads(causal_conv(lin_k, rim_k, conv_k, positions, segment, doc_lengths), DK)
    values = causal_conv(lin_v, rim_v, conv_v, positions, segment, doc_lengths).reshape(
        row_count, -1, DV
    )
    head_count = values.shape[1]
    queries = jnp.repeat(queries, VALUE_HEADS // QKH, axis=1)
    keys_unit = jnp.repeat(keys_unit, VALUE_HEADS // QKH, axis=1)
    beta_gate = jax.nn.sigmoid(beta_logit)
    device_pair, baseline_output, complete_reach, eye_heads, zero_heads = delta_blocks(
        queries, keys_unit, values, beta_gate, log_decay, segment, starts
    )
    arriving_input = prefix_2(
        (device_pair[0], device_pair[1]), "seq", compose, (eye_heads, zero_heads)
    )
    delta_output = baseline_output + jnp.einsum(
        "dpjt,ptw->dpjw", complete_reach, arriving_input[1], precision=EXACT_PRECISION
    )
    delta_output = jnp.swapaxes(delta_output, 1, 2).reshape(row_count, head_count, DV)
    inverse_rms = lax.rsqrt(jnp.mean(delta_output * delta_output, axis=-1, keepdims=True) + 1e-06)
    gate_z = jax.nn.silu(lin_z.astype(jnp.float32).reshape(row_count, head_count, DV))
    delta_out = (
        (delta_output * inverse_rms * gate_z)
        .astype(jnp.bfloat16)
        .reshape(row_count, head_count * DV)
    )
    aq_local = attn_query.shape[1] // AD
    query_heads = attn_query.reshape(row_count, aq_local, AD)
    kv_head = lax.axis_index("head") * aq_local // (AQ // KVH)
    own_pair = lax.dynamic_index_in_dim(attn_kv, kv_head, axis=2, keepdims=False)
    score_scale = AD ** (-0.5)

    def absorb(running, kv_piece, first_row):
        row_top, row_total, accum = running
        piece_rows = kv_piece.shape[0]
        key_pos = first_row + jnp.arange(piece_rows, dtype=jnp.int32)
        key_seg = segment_ids(key_pos, doc_lengths)
        allowed = (
            (key_pos[None, :] <= positions[:, None])
            & (key_seg[None, :] == segment[:, None])
            & (key_pos[None, :] >= 0)
        )
        scores = (
            jnp.einsum(
                "qhd,kd->hqk", query_heads, kv_piece[:, 0], preferred_element_type=jnp.float32
            )
            * score_scale
        )
        masked = jnp.where(allowed[None], scores, NEGATIVE)
        new_top = jnp.maximum(row_top, jnp.max(masked, axis=-1))
        weights_f = jnp.where(allowed[None], jnp.exp(masked - new_top[..., None]), 0.0)
        rescale = jnp.exp(row_top - new_top)
        row_total = row_total * rescale + jnp.sum(weights_f, axis=-1)
        accum = accum * rescale[..., None] + jnp.einsum(
            "hqk,kd->hqd",
            weights_f.astype(jnp.bfloat16),
            kv_piece[:, 1],
            preferred_element_type=jnp.float32,
        )
        return (new_top, row_total, accum)

    start_state = (
        jnp.full((aq_local, row_count), NEGATIVE, jnp.float32),
        jnp.zeros((aq_local, row_count), jnp.float32),
        jnp.zeros((aq_local, row_count, AD), jnp.float32),
    )
    running = absorb(start_state, own_pair, seq_index * row_count)

    def hop(hop_step, loop_state):
        loop_running, kv_piece = loop_state
        kv_piece = passed_along(kv_piece, "seq", 1)
        loop_running = absorb(loop_running, kv_piece, (seq_index - hop_step - 1) * row_count)
        return (loop_running, kv_piece)

    running, _ = lax.fori_loop(0, lax.axis_size("seq") // 4, hop, (running, own_pair))
    row_top, row_total, accum = running
    attended = jnp.swapaxes(accum / row_total[..., None], 0, 1).reshape(row_count, aq_local * AD)
    attn_out = (attended * jax.nn.sigmoid(attn_gate.astype(jnp.float32))).astype(jnp.bfloat16)
    return (delta_out, attn_out)


BF = jnp.bfloat16
F32 = jnp.float32
LANES = 128
LOG2E = 1.4426950408889634


def mm(a, b, transposed=False):
    contract = ((1,), (1,)) if transposed else ((1,), (0,))
    return lax.dot_general(a, b, (contract, ((), ())), preferred_element_type=F32)


def halves(x):
    high = x.astype(BF)
    return high, (x - high.astype(F32)).astype(BF)


def block_diagonal(wide):
    zero = jnp.zeros((wide.shape[0], LANES), wide.dtype)
    return jnp.concatenate(
        [
            jnp.concatenate([wide[:, :LANES], zero], axis=1),
            jnp.concatenate([zero, wide[:, LANES:]], axis=1),
        ],
        axis=0,
    )


def twice(x):
    return jnp.concatenate([x, x], axis=1)


def half_sigmoid(x):
    return 0.5 + 0.5 * jnp.tanh(0.5 * x)


def fused_kernel(
    count,
    doc_hbm,
    kv_hbm,
    q_hbm,
    k_hbm,
    v_hbm,
    conv_q_hbm,
    conv_k_hbm,
    conv_v_hbm,
    z_hbm,
    beta_hbm,
    decay_hbm,
    aq_hbm,
    ag_hbm,
    delta_out,
    attn_out,
    doc_ref,
    kv_raw,
    lin_q,
    lin_k,
    lin_v,
    conv_q,
    conv_k,
    conv_v,
    lin_z,
    beta_logit,
    log_decay,
    attn_query,
    attn_gate,
    rim_q,
    rim_k,
    rim_v,
    kv_own,
    kv_before,
    state_out,
    state_in,
    spread,
    local_out,
    reach_out,
    load_sem,
    send_sem,
    recv_sem,
):
    rows = lin_q.shape[0]
    heads = lin_v.shape[1] // DV
    pairs = range(lin_k.shape[1] // DK)
    docs = doc_ref.shape[0]
    rim = rim_q.shape[0]
    index = lax.axis_index("seq")
    head_index = lax.axis_index("head")
    lane_of_pair = lax.rem(head_index, 2)
    sibling = head_index + 1 - 2 * lane_of_pair
    aq_local = attn_query.shape[1] // AD
    kv_head = head_index * aq_local // (AQ // KVH)
    barrier = pltpu.get_barrier_semaphore()
    mesh_id = pl.DeviceIdType.MESH

    @pl.when(index > 0)
    def _():
        pl.semaphore_signal(
            barrier, inc=1, device_id={"seq": index - 1}, device_id_type=mesh_id
        )
        pl.semaphore_signal(
            barrier, inc=1, device_id={"head": sibling}, device_id_type=mesh_id
        )

    loads = {}

    def load(name, source, target):
        copy = pltpu.make_async_copy(source, target, load_sem.at[len(loads)])
        copy.start()
        loads[name] = copy

    load("doc", doc_hbm, doc_ref)
    load("decay", decay_hbm, log_decay)
    load("beta", beta_hbm, beta_logit)
    load("k", k_hbm, lin_k)
    load("conv_k", conv_k_hbm, conv_k)
    load("v", v_hbm, lin_v)
    load("conv_v", conv_v_hbm, conv_v)
    for side in range(2):
        for at in range(AD // LANES):
            load(
                ("kv", side, at),
                kv_hbm.at[:, side, :, pl.ds(at * LANES, LANES)],
                kv_raw.at[side * (AD // LANES) + at],
            )
    load("q", q_hbm, lin_q)
    load("conv_q", conv_q_hbm, conv_q)
    load("aq", aq_hbm, attn_query)
    load("ag", ag_hbm, attn_gate)
    load("z", z_hbm, lin_z)

    def remote(source, target, slot, where):
        return pltpu.make_async_remote_copy(
            src_ref=source,
            dst_ref=target,
            send_sem=send_sem.at[slot],
            recv_sem=recv_sem.at[slot],
            device_id=where,
            device_id_type=mesh_id,
        )

    ahead = {"seq": index + 1}
    tail = pl.ds(rows - rim, rim)
    rims = [
        remote(k_hbm.at[tail, :], rim_k, 0, ahead),
        remote(v_hbm.at[tail, :], rim_v, 1, ahead),
        remote(q_hbm.at[tail, :], rim_q, 2, ahead),
    ]
    kv_ahead = remote(kv_own.at[lane_of_pair], kv_before.at[lane_of_pair], 3, ahead)
    kv_across = remote(
        kv_before.at[lane_of_pair], kv_before.at[lane_of_pair], 4, {"head": sibling}
    )
    states = [
        remote(state_out.at[pl.ds(2 * p, 2)], state_in.at[pl.ds(2 * p, 2)], 5 + p, ahead)
        for p in pairs
    ]

    @pl.when((index > 0) & (index < count - 1))
    def _():
        pl.semaphore_wait(barrier, 2)

    @pl.when((index == 0) | (index == count - 1))
    def _():
        pl.semaphore_wait(barrier, 1)

    @pl.when(index < count - 1)
    def _():
        for copy in rims:
            copy.start()

    @pl.when(index == 0)
    def _():
        rim_q[...] = jnp.zeros_like(rim_q)
        rim_k[...] = jnp.zeros_like(rim_k)
        rim_v[...] = jnp.zeros_like(rim_v)
        kv_before[...] = jnp.zeros_like(kv_before)
        state_in[...] = jnp.zeros_like(state_in)

    def arrived(*copies):
        @pl.when(index > 0)
        def _():
            for copy in copies:
                copy.wait_recv()

    def loaded(*names):
        for name in names:
            loads[name].wait()

    loaded("doc", "decay", "beta")
    first = index * rows
    offset = -first
    offsets = [offset]
    for d in range(docs - 1):
        offset = offset + doc_ref[d]
        offsets.append(offset)

    def begins(position):
        begin = jnp.full(position.shape, offsets[0], jnp.int32)
        for offset in offsets[1:]:
            begin = jnp.where(position >= offset, offset, begin)
        return begin

    square = (rows, rows)
    row_id = lax.broadcasted_iota(jnp.int32, square, 0)
    col_id = lax.broadcasted_iota(jnp.int32, square, 1)
    row_begin = begins(row_id)
    inside = col_id >= row_begin
    strict = jnp.where((row_id > col_id) & inside, 1.0, 0.0)
    visible = (row_id >= col_id) & inside
    visible_before = col_id - rows >= row_begin
    same = [None] + [jnp.where(row_id - s >= row_begin, 1.0, 0.0) for s in (1, 2, 3)]
    short_id = lax.broadcasted_iota(jnp.int32, (heads, rows), 1)
    short_begin = begins(short_id)
    last_begin = begins(jnp.full((heads, rows), rows - 1, jnp.int32))

    rates = log_decay[...]
    part_a = rates.astype(BF)
    rest = rates - part_a.astype(F32)
    part_b = rest.astype(BF)
    part_c = (rest - part_b.astype(F32)).astype(BF)
    upper = jnp.where(row_id <= col_id, 1.0, 0.0).astype(BF)
    summed = (mm(part_a, upper) + mm(part_b, upper) + mm(part_c, upper)) * LOG2E
    beta_log = -jnp.log2(1.0 + jnp.exp(-beta_logit[...]))
    from_row = summed - beta_log
    carried_row = jnp.where(short_begin < 0, jnp.exp2(summed), 0.0)
    closing_row = jnp.where(
        short_id >= last_begin,
        jnp.exp2(summed[:, rows - 1 : rows] - from_row),
        0.0,
    )
    columns = jnp.concatenate(
        [summed, carried_row, closing_row, jnp.zeros((rows - 3 * heads, rows), F32)], axis=0
    ).T
    carried = [columns[:, heads + h : heads + h + 1] for h in range(heads)]
    closing = [columns[:, 2 * heads + h : 2 * heads + h + 1] for h in range(heads)]

    def decays(h):
        return jnp.exp2(jnp.minimum(columns[:, h : h + 1] - from_row[h : h + 1, :], 0.0))

    def conv(values, rim_ref, taps, at, slot):
        width = pl.ds(at * LANES, LANES)
        own = values[:, width].astype(F32)
        spread[slot, 0:8, :] = rim_ref[:, width].astype(F32)[rim - 8 :]
        spread[slot, 8 : 8 + rows, :] = own
        scale = taps[:, width].astype(F32) * 0.5
        total = own * scale[3:4]
        for s in (1, 2, 3):
            total = total + spread[slot, 8 - s : 8 - s + rows, :] * (
                scale[3 - s : 4 - s] * same[s]
            )
        return total + total * jnp.tanh(total)

    def unit(x):
        return x * lax.rsqrt(jnp.sum(x * x, axis=1, keepdims=True) + 1e-06)

    base = 8
    near = jnp.where(twice((row_id // base) == (col_id // base)), -1.0, 0.0).astype(BF)
    eye = jnp.where(twice(row_id == col_id), 1.0, 0.0).astype(BF)
    joints = []
    size = base
    while size < rows:
        joints.append(
            jnp.where(
                twice(
                    ((row_id // (2 * size)) == (col_id // (2 * size)))
                    & ((row_id // size) != (col_id // size))
                ),
                1.0,
                0.0,
            ).astype(BF)
        )
        size *= 2

    loaded("k", "conv_k")
    arrived(rims[0])

    keys, key_high, decay, corrector, values_of, moved = {}, {}, {}, {}, {}, {}

    def chain(p):
        keys[p] = unit(conv(lin_k, rim_k, conv_k, p, p))
        key_high[p] = keys[p].astype(BF)
        product = mm(key_high[p], key_high[p], transposed=True) * strict
        for h in (2 * p, 2 * p + 1):
            decay[h] = decays(h)
        lower = jnp.concatenate(
            [decay[2 * p] * product, decay[2 * p + 1] * product], axis=1
        ).astype(BF)
        yield
        power = lower * near
        square_of = mm(power, block_diagonal(power)).astype(BF)
        key_turned = keys[p].T.astype(BF)
        yield
        both = mm(jnp.concatenate([square_of, power], axis=0), block_diagonal(square_of))
        whole = power.astype(F32) + square_of.astype(F32) + both[rows:]
        fourth = both[:rows].astype(BF)
        yield
        whole = whole + fourth.astype(F32) + mm(whole.astype(BF), block_diagonal(fourth))
        inverse = eye + whole.astype(BF)
        for joint in joints:
            yield
            middle = mm(inverse, block_diagonal(lower * joint)).astype(BF)
            yield
            inverse = inverse - mm(middle, block_diagonal(inverse)).astype(BF)
        corrector[p] = inverse - eye
        yield
        wide = jnp.concatenate([values_of[2 * p], values_of[2 * p + 1]], axis=1)
        moved[p] = wide + mm(corrector[p], block_diagonal(wide.astype(BF)))
        ending = jnp.concatenate(
            [
                closing[2 * p] * moved[p][:, :DV],
                closing[2 * p + 1] * moved[p][:, DV:],
            ],
            axis=1,
        ).astype(BF)
        yield
        made = mm(key_turned, ending).astype(BF)
        state_out[2 * p] = made[:, :DV]
        state_out[2 * p + 1] = made[:, DV:]

        @pl.when(index < count - 1)
        def _():
            states[p].start()

    def prepare_values():
        loaded("v", "conv_v")
        arrived(rims[1])
        for h in range(heads):
            values_of[h] = conv(lin_v, rim_v, conv_v, h, len(pairs) + h)
            yield

    def choose_kv():
        loaded(*[("kv", side, at) for side in range(2) for at in range(AD // LANES)])
        choice = jnp.where(
            lax.broadcasted_iota(jnp.int32, (rows, 2 * rows), 1)
            == 2 * lax.broadcasted_iota(jnp.int32, (rows, 2 * rows), 0) + kv_head,
            1.0,
            0.0,
        ).astype(BF)
        flat = kv_raw.reshape(2 * AD // LANES, 2 * rows, LANES)
        for side in range(2):
            parts = [flat[side * (AD // LANES) + at] for at in range(AD // LANES)]
            kv_own[side] = mm(choice, jnp.concatenate(parts, axis=1)).astype(BF)

        @pl.when(index < count - 1)
        def _():
            kv_ahead.start()

    choose_kv()
    filler = prepare_values()
    chains = [chain(p) for p in pairs]
    skew = SKEW
    step = 0
    done = set()
    while len(done) < len(chains):
        for p in pairs:
            if p not in done and step >= p * skew:
                if next(chains[p], "end") == "end":
                    done.add(p)
        if step >= FILL_FROM:
            next(filler, None)
        step += 1

    arrived(kv_ahead)

    @pl.when(index > 0)
    def _():
        kv_across.start()

    loaded("q", "conv_q", "aq", "ag", "z")
    arrived(rims[2])

    for p in pairs:
        query = unit(conv(lin_q, rim_q, conv_q, p, len(pairs) + heads + p)) * DK ** (-0.5)
        high, low = halves(query)
        key_low = (keys[p] - key_high[p].astype(F32)).astype(BF)
        product = mm(
            jnp.concatenate([high, low, high], axis=1),
            jnp.concatenate([key_high[p], key_high[p], key_low], axis=1),
            transposed=True,
        )
        product = jnp.where(visible, product, 0.0)
        wide = jnp.concatenate(
            [carried[2 * p] * keys[p], carried[2 * p + 1] * keys[p]], axis=1
        )
        moved_keys = (wide + mm(corrector[p], block_diagonal(wide.astype(BF)))).astype(BF)
        values_high, values_low = halves(moved[p])
        for half in range(2):
            h = 2 * p + half
            lanes = slice(half * LANES, (half + 1) * LANES)
            high, low = halves(decay[h] * product)
            right = jnp.concatenate([values_high[:, lanes], moved_keys[:, lanes]], axis=1)
            mixed = mm(
                jnp.concatenate([high, low], axis=1), jnp.concatenate([right, right], axis=0)
            )
            local_out[h] = mixed[:, :DV] + mm(high, values_low[:, lanes])
            reach_out[h] = (carried[h] * query - mixed[:, DV:]).astype(BF)

    arrived(kv_across)
    allowed = jnp.concatenate([visible_before, visible], axis=1)
    all_keys = jnp.concatenate([kv_before[0], kv_own[0]], axis=0)
    all_values = jnp.concatenate([kv_before[1], kv_own[1]], axis=0)
    score_scale = AD ** (-0.5) * LOG2E
    for a in range(aq_local):
        width = pl.ds(a * AD, AD)
        scores = mm(attn_query[:, width], all_keys, transposed=True)
        masked = jnp.where(allowed, scores, NEGATIVE)
        top = jnp.max(masked, axis=1, keepdims=True)
        weights = jnp.exp2((masked - top) * score_scale)
        total = jnp.sum(weights, axis=1, keepdims=True)
        mixture = mm(weights.astype(BF), all_values)
        gate = half_sigmoid(attn_gate[:, width].astype(F32))
        attn_out[:, width] = (mixture * (1.0 / total) * gate).astype(BF)

    for p in pairs:
        arrived(states[p])
        for h in (2 * p, 2 * p + 1):
            gate = lin_z[:, pl.ds(h * DV, DV)].astype(F32) * 0.5
            gate = gate + gate * jnp.tanh(gate)
            value = local_out[h] + mm(reach_out[h], state_in[h])
            scale = lax.rsqrt(jnp.mean(value * value, axis=1, keepdims=True) + 1e-06)
            delta_out[:, pl.ds(h * DV, DV)] = (value * scale * gate).astype(BF)

    @pl.when(index < count - 1)
    def _():
        for copy in rims + [kv_ahead] + states:
            copy.wait_send()

    @pl.when(index > 0)
    def _():
        kv_across.wait_send()


KERNEL_BYTES = 62000000
SKEW = 0
FILL_FROM = 1


def deliver_kernel(delta_ref, attn_ref, delta_out, attn_out, sem):
    copies = [
        pltpu.make_async_copy(attn_ref, attn_out, sem.at[0]),
        pltpu.make_async_copy(delta_ref, delta_out, sem.at[1]),
    ]
    for copy in copies:
        copy.start()
    for copy in copies:
        copy.wait()


def fused(
    lin_q,
    lin_k,
    lin_v,
    conv_q,
    conv_k,
    conv_v,
    lin_z,
    beta_logit,
    log_decay,
    attn_query,
    attn_gate,
    attn_kv,
    doc_lengths,
):
    rows = lin_q.shape[0]
    heads = lin_v.shape[1] // DV
    pair_count = lin_k.shape[1] // DK
    streamed = (
        lin_q,
        lin_k,
        lin_v,
        conv_q,
        conv_k,
        conv_v,
        lin_z,
        beta_logit.T,
        log_decay.T,
        attn_query,
        attn_gate,
    )
    vmem = pl.BlockSpec(memory_space=pltpu.VMEM)
    hbm = pl.BlockSpec(memory_space=pltpu.HBM)
    rim = 16
    outs = (
        jax.ShapeDtypeStruct(lin_z.shape, BF),
        jax.ShapeDtypeStruct(attn_query.shape, BF),
    )
    lane_parts = 2 * AD // LANES
    delta, attn = pl.pallas_call(
        functools.partial(fused_kernel, lax.axis_size("seq")),
        out_shape=(pltpu.VMEM(lin_z.shape, BF), pltpu.VMEM(attn_query.shape, BF)),
        in_specs=[hbm] * 13,
        out_specs=(vmem, vmem),
        scratch_shapes=[
            pltpu.SMEM(doc_lengths.shape, jnp.int32),
            pltpu.VMEM((lane_parts, rows, KVH, LANES), BF),
        ]
        + [pltpu.VMEM(x.shape, x.dtype) for x in streamed]
        + [
            pltpu.VMEM((rim, lin_q.shape[1]), BF),
            pltpu.VMEM((rim, lin_k.shape[1]), BF),
            pltpu.VMEM((rim, lin_v.shape[1]), BF),
            pltpu.VMEM((2, rows, AD), BF),
            pltpu.VMEM((2, rows, AD), BF),
            pltpu.VMEM((heads, DK, DV), BF),
            pltpu.VMEM((heads, DK, DV), BF),
            pltpu.VMEM((2 * pair_count + heads, rows + 8, LANES), F32),
            pltpu.VMEM((heads, rows, DV), F32),
            pltpu.VMEM((heads, rows, DK), BF),
            pltpu.SemaphoreType.DMA((12 + lane_parts,)),
            pltpu.SemaphoreType.DMA((5 + pair_count,)),
            pltpu.SemaphoreType.DMA((5 + pair_count,)),
        ],
        compiler_params=pltpu.CompilerParams(
            collective_id=0, has_side_effects=True, vmem_limit_bytes=KERNEL_BYTES
        ),
    )(doc_lengths, attn_kv, *streamed)
    return pl.pallas_call(
        deliver_kernel,
        out_shape=outs,
        in_specs=[vmem, vmem],
        out_specs=(hbm, hbm),
        scratch_shapes=[pltpu.SemaphoreType.DMA((2,))],
        compiler_params=pltpu.CompilerParams(vmem_limit_bytes=1 << 20),
    )(delta, attn)


def solution(mesh):
    near = mesh.shape["seq"] == 4
    return jax.shard_map(
        fused if near else shards,
        mesh=mesh,
        in_specs=(
            P(("grp", "seq"), "head"),
            P(("grp", "seq"), "head"),
            P(("grp", "seq"), "head"),
            P(None, "head"),
            P(None, "head"),
            P(None, "head"),
            P(("grp", "seq"), "head"),
            P(("grp", "seq"), "head"),
            P(("grp", "seq"), "head"),
            P(("grp", "seq"), "head"),
            P(("grp", "seq"), "head"),
            P(("grp", "seq"), None, None, None),
            P("grp"),
        ),
        out_specs=(P(("grp", "seq"), "head"), P(("grp", "seq"), "head")),
        check_vma=False,
    )
```

```python
import functools

import jax
import jax.numpy as jnp
from jax import lax
from jax.experimental import pallas as pl
from jax.experimental.pallas import tpu as pltpu
from jax.sharding import PartitionSpec as P

DK = 128
DV = 128
QKH = 16
VALUE_HEADS = 32
AQ = 16
KVH = 2
AD = 256
BLOCK = 64


EXACT_PRECISION = lax.Precision.HIGHEST
NEGATIVE = -1e30


def passed_along(value, axis, steps):
    count = lax.axis_size(axis)
    initial, last = (max(0, -steps), min(count, count - steps))
    return lax.ppermute(value, axis, [(source, source + steps) for source in range(initial, last)])


def prefix_2(value, axis, combine, identity):
    length, index = (lax.axis_size(axis), lax.axis_index(axis))
    everything = jax.tree.map(
        lambda part, kind: lax.all_gather(part.astype(kind), axis),
        value,
        (jnp.bfloat16, jnp.bfloat16),
    )
    start = jax.tree.map(
        lambda part, zero: jnp.broadcast_to(jnp.asarray(zero, part.dtype), part.shape),
        value,
        identity,
    )

    def step(k, before):
        reached = k < index
        new = combine(
            before, jax.tree.map(lambda part, own: part[k].astype(own.dtype), everything, value)
        )
        return jax.tree.map(lambda a, b: jnp.where(reached, a, b), new, before)

    return lax.fori_loop(0, length, step, start)


def running_sum(values):
    count = values.shape[-1]
    later = lax.broadcasted_iota(jnp.int32, (count, count), 0)
    earlier = lax.broadcasted_iota(jnp.int32, (count, count), 1)
    kept = jnp.where(later >= earlier, values[..., None, :], jnp.zeros((), values.dtype))
    return jnp.sum(kept, axis=-1)


def segment_ids(positions, doc_lengths):
    offsets = running_sum(doc_lengths) - doc_lengths
    return jnp.sum((offsets[None, :] <= positions[:, None]).astype(jnp.int32), axis=1)


def start_flags(positions, doc_lengths):
    offsets = running_sum(doc_lengths) - doc_lengths
    return jnp.any(offsets[None, :] == positions[:, None], axis=1)


def causal_conv(values, margin, weights, positions, segment, doc_lengths):
    row_count = values.shape[0]
    tap_count = weights.shape[0]
    extended = jnp.concatenate([margin, values], axis=0).astype(jnp.float32)
    conv_sum = jnp.zeros(values.shape, jnp.float32)
    for tap_index in range(tap_count):
        source = positions - (tap_count - 1) + tap_index
        inside = (segment_ids(source, doc_lengths) == segment).astype(jnp.float32)
        conv_sum = (
            conv_sum
            + extended[tap_index : tap_index + row_count]
            * weights[tap_index].astype(jnp.float32)[None, :]
            * inside[:, None]
        )
    return jax.nn.silu(conv_sum)


def unit_heads(values, head_size):
    shaped = values.reshape(values.shape[0], -1, head_size)
    return shaped * lax.rsqrt(jnp.sum(shaped * shaped, axis=-1, keepdims=True) + 1e-06)


def compose(first_pair, second_pair):
    joined_map = jnp.einsum(
        "hij,hjk->hik", second_pair[0], first_pair[0], precision=EXACT_PRECISION
    )
    joined_shift = (
        jnp.einsum("hij,hjk->hik", second_pair[0], first_pair[1], precision=EXACT_PRECISION)
        + second_pair[1]
    )
    return (joined_map, joined_shift)


def unit_lower_inverse(lower_part, block_len):
    identity = jnp.eye(block_len, dtype=jnp.float32)
    power = -lower_part
    inverse = identity + power
    for _ in range(max(block_len - 1, 1).bit_length() - 1):
        power = jnp.einsum("nhij,nhjk->nhik", power, power, precision=EXACT_PRECISION)
        inverse = jnp.einsum(
            "nhij,nhjk->nhik", inverse, identity + power, precision=EXACT_PRECISION
        )
    return inverse


def delta_blocks(queries, keys_unit, values, beta_gate, log_rates, segment, starts):
    row_count, head_count, key_size = keys_unit.shape
    value_size = values.shape[2]
    block_len = BLOCK
    block_count = row_count // block_len

    def to_blocks(array):
        return jnp.swapaxes(array.reshape((block_count, block_len) + array.shape[1:]), 1, 2)

    query_blk = to_blocks(queries)
    key_blk = to_blocks(keys_unit)
    value_blk = to_blocks(values)
    beta_blk = to_blocks(beta_gate)
    cumulative = running_sum(to_blocks(log_rates))
    segment_blk = segment.reshape(block_count, block_len)
    fresh_count = running_sum(starts.reshape(block_count, block_len).astype(jnp.int32))
    later_row = lax.broadcasted_iota(jnp.int32, (block_len, block_len), 0)
    earlier_col = lax.broadcasted_iota(jnp.int32, (block_len, block_len), 1)
    visible = (later_row >= earlier_col)[None] & (
        segment_blk[:, :, None] == segment_blk[:, None, :]
    )
    visible = visible[:, None]
    spread = cumulative[..., :, None] - cumulative[..., None, :]
    decay_mat = jnp.where(visible, jnp.exp(jnp.where(visible, spread, 0.0)), 0.0)
    carried = jnp.where((fresh_count == 0)[:, None, :], jnp.exp(cumulative), 0.0)
    key_key = jnp.einsum("nhik,nhjk->nhij", key_blk, key_blk, precision=EXACT_PRECISION)
    strict = (later_row > earlier_col).astype(jnp.float32)
    lower_part = decay_mat * strict * key_key * beta_blk[..., None, :]
    inverse = unit_lower_inverse(lower_part, block_len)
    right_side = jnp.concatenate([value_blk, carried[..., None] * key_blk], axis=-1)
    solved = jnp.einsum("nhij,nhjc->nhic", inverse, right_side, precision=EXACT_PRECISION)
    moved_values = solved[..., :value_size]
    moved_keys = solved[..., value_size:]
    query_key = jnp.einsum("nhik,nhjk->nhij", query_blk, key_blk, precision=EXACT_PRECISION)
    attend = decay_mat * query_key * beta_blk[..., None, :]
    out_zero = jnp.einsum("nhij,nhjv->nhiv", attend, moved_values, precision=EXACT_PRECISION)
    reach_part = carried[..., None] * query_blk - jnp.einsum(
        "nhij,nhjk->nhik", attend, moved_keys, precision=EXACT_PRECISION
    )
    weighted = (beta_blk * decay_mat[..., block_len - 1, :])[..., None] * key_blk
    block_map = carried[..., block_len - 1][..., None, None] * jnp.eye(
        key_size, dtype=jnp.float32
    ) - jnp.einsum("nhjk,nhjl->nhkl", weighted, moved_keys, precision=EXACT_PRECISION)
    block_shift = jnp.einsum("nhjk,nhjv->nhkv", weighted, moved_values, precision=EXACT_PRECISION)

    def advance(prefix, current):
        return (compose(prefix, current), prefix)

    eye_heads = jnp.broadcast_to(
        jnp.eye(key_size, dtype=jnp.float32), (head_count, key_size, key_size)
    )
    zero_heads = jnp.zeros((head_count, key_size, value_size), jnp.float32)
    device_pair, prefixes = lax.scan(advance, (eye_heads, zero_heads), (block_map, block_shift))
    baseline_output = out_zero + jnp.einsum(
        "nhik,nhkv->nhiv", reach_part, prefixes[1], precision=EXACT_PRECISION
    )
    complete_reach = jnp.einsum(
        "nhik,nhkl->nhil", reach_part, prefixes[0], precision=EXACT_PRECISION
    )
    return (device_pair, baseline_output, complete_reach, eye_heads, zero_heads)


def shards(
    lin_q,
    lin_k,
    lin_v,
    conv_q,
    conv_k,
    conv_v,
    lin_z,
    beta_logit,
    log_decay,
    attn_query,
    attn_gate,
    attn_kv,
    doc_lengths,
):
    row_count = lin_q.shape[0]
    seq_index = lax.axis_index("seq")
    positions = seq_index * row_count + jnp.arange(row_count, dtype=jnp.int32)
    segment = segment_ids(positions, doc_lengths)
    starts = start_flags(positions, doc_lengths)
    rim_from = row_count - conv_q.shape[0] + 1
    rim_q, rim_k, rim_v = passed_along(
        (lin_q[rim_from:], lin_k[rim_from:], lin_v[rim_from:]), "seq", 1
    )
    queries = unit_heads(
        causal_conv(lin_q, rim_q, conv_q, positions, segment, doc_lengths), DK
    ) * DK ** (-0.5)
    keys_unit = unit_heads(causal_conv(lin_k, rim_k, conv_k, positions, segment, doc_lengths), DK)
    values = causal_conv(lin_v, rim_v, conv_v, positions, segment, doc_lengths).reshape(
        row_count, -1, DV
    )
    head_count = values.shape[1]
    queries = jnp.repeat(queries, VALUE_HEADS // QKH, axis=1)
    keys_unit = jnp.repeat(keys_unit, VALUE_HEADS // QKH, axis=1)
    beta_gate = jax.nn.sigmoid(beta_logit)
    device_pair, baseline_output, complete_reach, eye_heads, zero_heads = delta_blocks(
        queries, keys_unit, values, beta_gate, log_decay, segment, starts
    )
    arriving_input = prefix_2(
        (device_pair[0], device_pair[1]), "seq", compose, (eye_heads, zero_heads)
    )
    delta_output = baseline_output + jnp.einsum(
        "dpjt,ptw->dpjw", complete_reach, arriving_input[1], precision=EXACT_PRECISION
    )
    delta_output = jnp.swapaxes(delta_output, 1, 2).reshape(row_count, head_count, DV)
    inverse_rms = lax.rsqrt(jnp.mean(delta_output * delta_output, axis=-1, keepdims=True) + 1e-06)
    gate_z = jax.nn.silu(lin_z.astype(jnp.float32).reshape(row_count, head_count, DV))
    delta_out = (
        (delta_output * inverse_rms * gate_z)
        .astype(jnp.bfloat16)
        .reshape(row_count, head_count * DV)
    )
    aq_local = attn_query.shape[1] // AD
    query_heads = attn_query.reshape(row_count, aq_local, AD)
    kv_head = lax.axis_index("head") * aq_local // (AQ // KVH)
    own_pair = lax.dynamic_index_in_dim(attn_kv, kv_head, axis=2, keepdims=False)
    score_scale = AD ** (-0.5)

    def absorb(running, kv_piece, first_row):
        row_top, row_total, accum = running
        piece_rows = kv_piece.shape[0]
        key_pos = first_row + jnp.arange(piece_rows, dtype=jnp.int32)
        key_seg = segment_ids(key_pos, doc_lengths)
        allowed = (
            (key_pos[None, :] <= positions[:, None])
            & (key_seg[None, :] == segment[:, None])
            & (key_pos[None, :] >= 0)
        )
        scores = (
            jnp.einsum(
                "qhd,kd->hqk", query_heads, kv_piece[:, 0], preferred_element_type=jnp.float32
            )
            * score_scale
        )
        masked = jnp.where(allowed[None], scores, NEGATIVE)
        new_top = jnp.maximum(row_top, jnp.max(masked, axis=-1))
        weights_f = jnp.where(allowed[None], jnp.exp(masked - new_top[..., None]), 0.0)
        rescale = jnp.exp(row_top - new_top)
        row_total = row_total * rescale + jnp.sum(weights_f, axis=-1)
        accum = accum * rescale[..., None] + jnp.einsum(
            "hqk,kd->hqd",
            weights_f.astype(jnp.bfloat16),
            kv_piece[:, 1],
            preferred_element_type=jnp.float32,
        )
        return (new_top, row_total, accum)

    start_state = (
        jnp.full((aq_local, row_count), NEGATIVE, jnp.float32),
        jnp.zeros((aq_local, row_count), jnp.float32),
        jnp.zeros((aq_local, row_count, AD), jnp.float32),
    )
    running = absorb(start_state, own_pair, seq_index * row_count)

    def hop(hop_step, loop_state):
        loop_running, kv_piece = loop_state
        kv_piece = passed_along(kv_piece, "seq", 1)
        loop_running = absorb(loop_running, kv_piece, (seq_index - hop_step - 1) * row_count)
        return (loop_running, kv_piece)

    running, _ = lax.fori_loop(0, lax.axis_size("seq") // 4, hop, (running, own_pair))
    row_top, row_total, accum = running
    attended = jnp.swapaxes(accum / row_total[..., None], 0, 1).reshape(row_count, aq_local * AD)
    attn_out = (attended * jax.nn.sigmoid(attn_gate.astype(jnp.float32))).astype(jnp.bfloat16)
    return (delta_out, attn_out)


BF = jnp.bfloat16
F32 = jnp.float32
LANES = 128
LOG2E = 1.4426950408889634


def mm(a, b, transposed=False):
    contract = ((1,), (1,)) if transposed else ((1,), (0,))
    return lax.dot_general(a, b, (contract, ((), ())), preferred_element_type=F32)


def halves(x):
    high = x.astype(BF)
    return high, (x - high.astype(F32)).astype(BF)


def block_diagonal(wide):
    zero = jnp.zeros((wide.shape[0], LANES), wide.dtype)
    return jnp.concatenate(
        [
            jnp.concatenate([wide[:, :LANES], zero], axis=1),
            jnp.concatenate([zero, wide[:, LANES:]], axis=1),
        ],
        axis=0,
    )


def twice(x):
    return jnp.concatenate([x, x], axis=1)


def half_sigmoid(x):
    return 0.5 + 0.5 * jnp.tanh(0.5 * x)


def fused_kernel(
    count,
    doc_hbm,
    kv_hbm,
    q_hbm,
    k_hbm,
    v_hbm,
    conv_q_hbm,
    conv_k_hbm,
    conv_v_hbm,
    z_hbm,
    beta_hbm,
    decay_hbm,
    aq_hbm,
    ag_hbm,
    delta_out,
    attn_out,
    doc_ref,
    kv_raw,
    lin_q,
    lin_k,
    lin_v,
    conv_q,
    conv_k,
    conv_v,
    lin_z,
    beta_logit,
    log_decay,
    attn_query,
    attn_gate,
    rim_q,
    rim_k,
    rim_v,
    kv_own,
    kv_before,
    state_out,
    state_in,
    spread,
    local_out,
    reach_out,
    gates,
    load_sem,
    send_sem,
    recv_sem,
):
    rows = lin_q.shape[0]
    heads = lin_v.shape[1] // DV
    pairs = range(lin_k.shape[1] // DK)
    docs = doc_ref.shape[0]
    rim = rim_q.shape[0]
    index = lax.axis_index("seq")
    head_index = lax.axis_index("head")
    lane_of_pair = lax.rem(head_index, 2)
    sibling = head_index + 1 - 2 * lane_of_pair
    aq_local = attn_query.shape[1] // AD
    kv_head = head_index * aq_local // (AQ // KVH)
    barrier = pltpu.get_barrier_semaphore()
    mesh_id = pl.DeviceIdType.MESH

    @pl.when(index > 0)
    def _():
        pl.semaphore_signal(
            barrier, inc=1, device_id={"seq": index - 1}, device_id_type=mesh_id
        )
        pl.semaphore_signal(
            barrier, inc=1, device_id={"head": sibling}, device_id_type=mesh_id
        )

    loads = {}

    def load(name, source, target):
        copy = pltpu.make_async_copy(source, target, load_sem.at[len(loads)])
        copy.start()
        loads[name] = copy

    load("doc", doc_hbm, doc_ref)
    load("decay", decay_hbm, log_decay)
    load("beta", beta_hbm, beta_logit)
    load("k", k_hbm, lin_k)
    load("conv_k", conv_k_hbm, conv_k)
    load("v", v_hbm, lin_v)
    load("conv_v", conv_v_hbm, conv_v)
    for side in range(2):
        for at in range(AD // LANES):
            load(
                ("kv", side, at),
                kv_hbm.at[:, side, :, pl.ds(at * LANES, LANES)],
                kv_raw.at[side * (AD // LANES) + at],
            )
    load("q", q_hbm, lin_q)
    load("conv_q", conv_q_hbm, conv_q)
    load("aq", aq_hbm, attn_query)
    load("ag", ag_hbm, attn_gate)
    load("z", z_hbm, lin_z)

    def remote(source, target, slot, where):
        return pltpu.make_async_remote_copy(
            src_ref=source,
            dst_ref=target,
            send_sem=send_sem.at[slot],
            recv_sem=recv_sem.at[slot],
            device_id=where,
            device_id_type=mesh_id,
        )

    ahead = {"seq": index + 1}
    tail = pl.ds(rows - rim, rim)
    rims = [
        remote(k_hbm.at[tail, :], rim_k, 0, ahead),
        remote(v_hbm.at[tail, :], rim_v, 1, ahead),
        remote(q_hbm.at[tail, :], rim_q, 2, ahead),
    ]
    kv_ahead = remote(kv_own.at[lane_of_pair], kv_before.at[lane_of_pair], 3, ahead)
    kv_across = remote(
        kv_before.at[lane_of_pair], kv_before.at[lane_of_pair], 4, {"head": sibling}
    )
    states = [
        remote(state_out.at[pl.ds(2 * p, 2)], state_in.at[pl.ds(2 * p, 2)], 5 + p, ahead)
        for p in pairs
    ]

    @pl.when(index == 0)
    def _():
        rim_q[...] = jnp.zeros_like(rim_q)
        rim_k[...] = jnp.zeros_like(rim_k)
        rim_v[...] = jnp.zeros_like(rim_v)
        kv_before[...] = jnp.zeros_like(kv_before)
        state_in[...] = jnp.zeros_like(state_in)

    def arrived(*copies):
        @pl.when(index > 0)
        def _():
            for copy in copies:
                copy.wait_recv()

    def loaded(*names):
        for name in names:
            loads[name].wait()

    @pl.when((index > 0) & (index < count - 1))
    def _():
        pl.semaphore_wait(barrier, 2)

    @pl.when((index == 0) | (index == count - 1))
    def _():
        pl.semaphore_wait(barrier, 1)

    @pl.when(index < count - 1)
    def _():
        for copy in rims[:2]:
            copy.start()

    loaded("doc")
    first = index * rows
    offset = -first
    offsets = [offset]
    for d in range(docs - 1):
        offset = offset + doc_ref[d]
        offsets.append(offset)

    def begins(position):
        begin = jnp.full(position.shape, offsets[0], jnp.int32)
        for offset in offsets[1:]:
            begin = jnp.where(position >= offset, offset, begin)
        return begin

    square = (rows, rows)
    row_id = lax.broadcasted_iota(jnp.int32, square, 0)
    col_id = lax.broadcasted_iota(jnp.int32, square, 1)
    row_begin = begins(row_id)
    inside = col_id >= row_begin
    strict = jnp.where((row_id > col_id) & inside, 1.0, 0.0)
    visible = (row_id >= col_id) & inside
    visible_before = col_id - rows >= row_begin
    same = [None] + [jnp.where(row_id - s >= row_begin, 1.0, 0.0) for s in (1, 2, 3)]
    short_id = lax.broadcasted_iota(jnp.int32, (heads, rows), 1)
    short_begin = begins(short_id)
    last_begin = begins(jnp.full((heads, rows), rows - 1, jnp.int32))

    loaded("decay", "beta")
    rates = log_decay[...]
    part_a = rates.astype(BF)
    rest = rates - part_a.astype(F32)
    part_b = rest.astype(BF)
    part_c = (rest - part_b.astype(F32)).astype(BF)
    upper = jnp.where(row_id <= col_id, 1.0, 0.0).astype(BF)
    summed = (mm(part_a, upper) + mm(part_b, upper) + mm(part_c, upper)) * LOG2E
    beta_log = -jnp.log2(1.0 + jnp.exp(-beta_logit[...]))
    from_row = summed - beta_log
    carried_row = jnp.where(short_begin < 0, jnp.exp2(summed), 0.0)
    closing_row = jnp.where(
        short_id >= last_begin,
        jnp.exp2(summed[:, rows - 1 : rows] - from_row),
        0.0,
    )
    columns = jnp.concatenate(
        [summed, carried_row, closing_row, jnp.zeros((rows - 3 * heads, rows), F32)], axis=0
    ).T
    carried = [columns[:, heads + h : heads + h + 1] for h in range(heads)]
    closing = [columns[:, 2 * heads + h : 2 * heads + h + 1] for h in range(heads)]

    def decays(h):
        return jnp.exp2(jnp.minimum(columns[:, h : h + 1] - from_row[h : h + 1, :], 0.0))

    def unit(x):
        return x * lax.rsqrt(jnp.sum(x * x, axis=1, keepdims=True) + 1e-06)

    def plain(x):
        return x

    def conv(values, rim_ref, taps, at, slot, finish):
        width = pl.ds(at * LANES, LANES)
        scale = taps[:, width].astype(F32) * 0.5
        weights = [scale[3:4]] + [scale[3 - s : 4 - s] * same[s] for s in (1, 2, 3)]

        def silu(own, begin, end):
            total = own * weights[0]
            for s in (1, 2, 3):
                total = total + spread[slot, 8 + begin - s : 8 + end - s, :] * (
                    weights[s][begin:end]
                )
            return finish(total + total * jnp.tanh(total))

        own = values[:, width].astype(F32)
        spread[slot, 8 : 8 + rows, :] = own
        later = silu(own[8:], 8, rows)
        yield
        spread[slot, 0:8, :] = rim_ref[:, width].astype(F32)[rim - 8 :]
        yield jnp.concatenate([silu(own[:8], 0, 8), later], axis=0)

    base = 8
    near = jnp.where(twice((row_id // base) == (col_id // base)), -1.0, 0.0).astype(BF)
    eye = jnp.where(twice(row_id == col_id), 1.0, 0.0).astype(BF)
    joints = []
    size = base
    while size < rows:
        joints.append(
            jnp.where(
                twice(
                    ((row_id // (2 * size)) == (col_id // (2 * size)))
                    & ((row_id // size) != (col_id // size))
                ),
                1.0,
                0.0,
            ).astype(BF)
        )
        size *= 2

    convs = {}

    def begin_conv(kind, values, rim_ref, taps, at, slot, finish):
        convs[kind, at] = conv(values, rim_ref, taps, at, slot, finish)
        next(convs[kind, at])


    keys, key_high, decay, corrector, values_of, moved = {}, {}, {}, {}, {}, {}

    def chain(p):
        keys[p] = next(convs["k", p])
        key_high[p] = keys[p].astype(BF)
        product = mm(key_high[p], key_high[p], transposed=True) * strict
        lower = jnp.concatenate(
            [decay[2 * p] * product, decay[2 * p + 1] * product], axis=1
        ).astype(BF)
        yield
        power = lower * near
        square_of = mm(power, block_diagonal(power)).astype(BF)
        key_turned = keys[p].T.astype(BF)
        yield
        both = mm(jnp.concatenate([square_of, power], axis=0), block_diagonal(square_of))
        whole = power.astype(F32) + square_of.astype(F32) + both[rows:]
        fourth = both[:rows].astype(BF)
        yield
        whole = whole + fourth.astype(F32) + mm(whole.astype(BF), block_diagonal(fourth))
        inverse = eye + whole.astype(BF)
        for stage, joint in enumerate(joints):
            yield
            if stage in VALUES_AT:
                h = 2 * p + VALUES_AT.index(stage)
                if h % 2 >= EARLY_V:
                    begin_conv("v", lin_v, rim_v, conv_v, h, len(pairs) + h, plain)
                values_of[h] = next(convs["v", h])
            middle = mm(inverse, block_diagonal(lower * joint)).astype(BF)
            if stage + 1 < len(joints):
                yield
                inverse = inverse - mm(middle, block_diagonal(inverse)).astype(BF)
        corrector[p] = (inverse - eye, middle)
        wide = jnp.concatenate([values_of[2 * p], values_of[2 * p + 1]], axis=1)
        part = wide + mm(corrector[p][0], block_diagonal(wide.astype(BF)))
        yield
        moved[p] = part - mm(middle, block_diagonal(part.astype(BF)))
        ending = jnp.concatenate(
            [
                closing[2 * p] * moved[p][:, :DV],
                closing[2 * p + 1] * moved[p][:, DV:],
            ],
            axis=1,
        ).astype(BF)
        yield
        made = mm(key_turned, ending).astype(BF)
        state_out[2 * p] = made[:, :DV]
        state_out[2 * p + 1] = made[:, DV:]

        @pl.when(index < count - 1)
        def _():
            states[p].start()

    def choose_kv():
        choice = jnp.where(
            lax.broadcasted_iota(jnp.int32, (rows, 2 * rows), 1)
            == 2 * lax.broadcasted_iota(jnp.int32, (rows, 2 * rows), 0) + kv_head,
            1.0,
            0.0,
        ).astype(BF)
        flat = kv_raw.reshape(2 * AD // LANES, 2 * rows, LANES)
        for side in range(2):
            parts = [flat[side * (AD // LANES) + at] for at in range(AD // LANES)]
            kv_own[side] = mm(choice, jnp.concatenate(parts, axis=1)).astype(BF)

        @pl.when(index < count - 1)
        def _():
            kv_ahead.start()
            rims[2].start()

    def local(p):
        if QUERY_LATE:
            begin_conv("q", lin_q, rim_q, conv_q, p, len(pairs) + heads + p, unit)
        query = next(convs["q", p]) * DK ** (-0.5)
        high, low = halves(query)
        key_low = (keys[p] - key_high[p].astype(F32)).astype(BF)
        product = mm(
            jnp.concatenate([high, low, high], axis=1),
            jnp.concatenate([key_high[p], key_high[p], key_low], axis=1),
            transposed=True,
        )
        product = jnp.where(visible, product, 0.0)
        yield
        wide = jnp.concatenate(
            [carried[2 * p] * keys[p], carried[2 * p + 1] * keys[p]], axis=1
        )
        part = wide + mm(corrector[p][0], block_diagonal(wide.astype(BF)))
        moved_keys = (part - mm(corrector[p][1], block_diagonal(part.astype(BF)))).astype(BF)
        values_high, values_low = halves(moved[p])
        for half in range(2):
            yield
            h = 2 * p + half
            lanes = slice(half * LANES, (half + 1) * LANES)
            high, low = halves(decay[h] * product)
            right = jnp.concatenate([values_high[:, lanes], moved_keys[:, lanes]], axis=1)
            mixed = mm(
                jnp.concatenate([high, low], axis=1), jnp.concatenate([right, right], axis=0)
            )
            local_out[h] = mixed[:, :DV] + mm(high, values_low[:, lanes])
            reach_out[h] = (carried[h] * query - mixed[:, DV:]).astype(BF)

    def forward_kv():
        arrived(kv_ahead)

        @pl.when(index > 0)
        def _():
            kv_across.start()

    def attend(a):
        if a == 0:
            arrived(kv_across)
        allowed = jnp.concatenate([visible_before, visible], axis=1)
        all_keys = jnp.concatenate([kv_before[0], kv_own[0]], axis=0)
        width = pl.ds(a * AD, AD)
        scores = mm(attn_query[:, width], all_keys, transposed=True)
        masked = jnp.where(allowed, scores, NEGATIVE)
        top = jnp.max(masked, axis=1, keepdims=True)
        yield
        weights = jnp.exp2((masked - top) * (AD ** (-0.5) * LOG2E))
        total = jnp.sum(weights, axis=1, keepdims=True)
        gate = half_sigmoid(attn_gate[:, width].astype(F32)) * (1.0 / total)
        yield
        all_values = jnp.concatenate([kv_before[1], kv_own[1]], axis=0)
        attn_out[:, width] = (mm(weights.astype(BF), all_values) * gate).astype(BF)

    def gate_values(p):
        for h in (2 * p, 2 * p + 1):
            gate = lin_z[:, pl.ds(h * DV, DV)].astype(F32) * 0.5
            gates[h] = gate + gate * jnp.tanh(gate)

    loaded("k", "conv_k")
    for p in pairs:
        begin_conv("k", lin_k, rim_k, conv_k, p, p, unit)
    loaded("v", "conv_v")
    for h in range(heads):
        if h % 2 < EARLY_V:
            begin_conv("v", lin_v, rim_v, conv_v, h, len(pairs) + h, plain)
        decay[h] = decays(h)
    loaded(*[("kv", side, at) for side in range(2) for at in range(AD // LANES)])
    choose_kv()
    loaded("q", "conv_q", "aq", "ag", "z")
    for p in pairs:
        if not QUERY_LATE:
            begin_conv("q", lin_q, rim_q, conv_q, p, len(pairs) + heads + p, unit)
    for p in EARLY_GATES:
        gate_values(p)
    arrived(rims[0])
    chains = [chain(p) for p in pairs]
    locals_of = [local(p) for p in pairs]
    attends = [attend(a) for a in range(aq_local)]
    pieces = []
    for name in PIECES:
        kind, at = name[0], int(name[1])
        if kind == "q":
            pieces.append((0, functools.partial(next, locals_of[at], None)))
        elif kind == "m":
            pieces.append((STARTS[at] + 15, functools.partial(next, locals_of[at], None)))
        elif kind == "f":
            pieces.append((0, forward_kv))
        elif kind == "a":
            pieces.append((0, functools.partial(next, attends[at], None)))
        else:
            pieces.append((0, functools.partial(gate_values, at)))
    for step in range(max(STARTS) + 15):
        if step == TAIL_AT:
            arrived(rims[1])
        for p in pairs:
            if step >= STARTS[p]:
                next(chains[p], None)
        if step >= PIECES_FROM and (step - PIECES_FROM) % PIECES_EVERY == 0:
            ready = [item for item in pieces if item[0] <= step]
            if ready:
                pieces.remove(ready[0])
                ready[0][1]()
    arrived(rims[2])
    for _, piece in pieces:
        piece()

    for p in pairs:
        arrived(states[p])
        for h in (2 * p, 2 * p + 1):
            value = local_out[h] + mm(reach_out[h], state_in[h])
            scale = lax.rsqrt(jnp.mean(value * value, axis=1, keepdims=True) + 1e-06)
            delta_out[:, pl.ds(h * DV, DV)] = (value * scale * gates[h]).astype(BF)

    @pl.when(index < count - 1)
    def _():
        for copy in rims + [kv_ahead] + states:
            copy.wait_send()

    @pl.when(index > 0)
    def _():
        kv_across.wait_send()


PIECES = ("f0",) + tuple(
    kind + str(at) for kind in ("z", "q", "m", "m", "m", "a", "a", "a") for at in range(4)
)
KERNEL_BYTES = 62_000_000
QUERY_LATE = True
EARLY_GATES = ()
PIECES_FROM = 100
PIECES_EVERY = 1
STARTS = (0, 0, 0, 0)
VALUES_AT = (1, 2)
TAIL_AT = 6
EARLY_V = 1


def deliver_kernel(delta_ref, attn_ref, delta_out, attn_out, sem):
    copies = [
        pltpu.make_async_copy(attn_ref, attn_out, sem.at[0]),
        pltpu.make_async_copy(delta_ref, delta_out, sem.at[1]),
    ]
    for copy in copies:
        copy.start()
    for copy in copies:
        copy.wait()


def fused(
    lin_q,
    lin_k,
    lin_v,
    conv_q,
    conv_k,
    conv_v,
    lin_z,
    beta_logit,
    log_decay,
    attn_query,
    attn_gate,
    attn_kv,
    doc_lengths,
):
    rows = lin_q.shape[0]
    heads = lin_v.shape[1] // DV
    pair_count = lin_k.shape[1] // DK
    streamed = (
        lin_q,
        lin_k,
        lin_v,
        conv_q,
        conv_k,
        conv_v,
        lin_z,
        beta_logit.T,
        log_decay.T,
        attn_query,
        attn_gate,
    )
    vmem = pl.BlockSpec(memory_space=pltpu.VMEM)
    hbm = pl.BlockSpec(memory_space=pltpu.HBM)
    rim = 16
    outs = (
        jax.ShapeDtypeStruct(lin_z.shape, BF),
        jax.ShapeDtypeStruct(attn_query.shape, BF),
    )
    lane_parts = 2 * AD // LANES
    delta, attn = pl.pallas_call(
        functools.partial(fused_kernel, lax.axis_size("seq")),
        out_shape=(pltpu.VMEM(lin_z.shape, BF), pltpu.VMEM(attn_query.shape, BF)),
        in_specs=[hbm] * 13,
        out_specs=(vmem, vmem),
        scratch_shapes=[
            pltpu.SMEM(doc_lengths.shape, jnp.int32),
            pltpu.VMEM((lane_parts, rows, KVH, LANES), BF),
        ]
        + [pltpu.VMEM(x.shape, x.dtype) for x in streamed]
        + [
            pltpu.VMEM((rim, lin_q.shape[1]), BF),
            pltpu.VMEM((rim, lin_k.shape[1]), BF),
            pltpu.VMEM((rim, lin_v.shape[1]), BF),
            pltpu.VMEM((2, rows, AD), BF),
            pltpu.VMEM((2, rows, AD), BF),
            pltpu.VMEM((heads, DK, DV), BF),
            pltpu.VMEM((heads, DK, DV), BF),
            pltpu.VMEM((2 * pair_count + heads, rows + 8, LANES), F32),
            pltpu.VMEM((heads, rows, DV), F32),
            pltpu.VMEM((heads, rows, DK), BF),
            pltpu.VMEM((heads, rows, DV), F32),
            pltpu.SemaphoreType.DMA((12 + lane_parts,)),
            pltpu.SemaphoreType.DMA((5 + pair_count,)),
            pltpu.SemaphoreType.DMA((5 + pair_count,)),
        ],
        compiler_params=pltpu.CompilerParams(
            collective_id=0, has_side_effects=True, vmem_limit_bytes=KERNEL_BYTES
        ),
    )(doc_lengths, attn_kv, *streamed)
    return pl.pallas_call(
        deliver_kernel,
        out_shape=outs,
        in_specs=[vmem, vmem],
        out_specs=(hbm, hbm),
        scratch_shapes=[pltpu.SemaphoreType.DMA((2,))],
        compiler_params=pltpu.CompilerParams(vmem_limit_bytes=1 << 20),
    )(delta, attn)


def solution(mesh):
    near = mesh.shape["seq"] == 4
    return jax.shard_map(
        fused if near else shards,
        mesh=mesh,
        in_specs=(
            P(("grp", "seq"), "head"),
            P(("grp", "seq"), "head"),
            P(("grp", "seq"), "head"),
            P(None, "head"),
            P(None, "head"),
            P(None, "head"),
            P(("grp", "seq"), "head"),
            P(("grp", "seq"), "head"),
            P(("grp", "seq"), "head"),
            P(("grp", "seq"), "head"),
            P(("grp", "seq"), "head"),
            P(("grp", "seq"), None, None, None),
            P("grp"),
        ),
        out_specs=(P(("grp", "seq"), "head"), P(("grp", "seq"), "head")),
        check_vma=False,
    )
```

```python
import functools

import jax
import jax.numpy as jnp
from jax import lax
from jax.experimental import pallas as pl
from jax.experimental.pallas import tpu as pltpu
from jax.sharding import PartitionSpec as P

DK = 128
DV = 128
QKH = 16
VALUE_HEADS = 32
AQ = 16
KVH = 2
AD = 256
BLOCK = 64


EXACT_PRECISION = lax.Precision.HIGHEST
NEGATIVE = -1e30


def passed_along(value, axis, steps):
    count = lax.axis_size(axis)
    initial, last = (max(0, -steps), min(count, count - steps))
    return lax.ppermute(value, axis, [(source, source + steps) for source in range(initial, last)])


def prefix_2(value, axis, combine, identity):
    length, index = (lax.axis_size(axis), lax.axis_index(axis))
    everything = jax.tree.map(
        lambda part, kind: lax.all_gather(part.astype(kind), axis),
        value,
        (jnp.bfloat16, jnp.bfloat16),
    )
    start = jax.tree.map(
        lambda part, zero: jnp.broadcast_to(jnp.asarray(zero, part.dtype), part.shape),
        value,
        identity,
    )

    def step(k, before):
        reached = k < index
        new = combine(
            before, jax.tree.map(lambda part, own: part[k].astype(own.dtype), everything, value)
        )
        return jax.tree.map(lambda a, b: jnp.where(reached, a, b), new, before)

    return lax.fori_loop(0, length, step, start)


def running_sum(values):
    count = values.shape[-1]
    later = lax.broadcasted_iota(jnp.int32, (count, count), 0)
    earlier = lax.broadcasted_iota(jnp.int32, (count, count), 1)
    kept = jnp.where(later >= earlier, values[..., None, :], jnp.zeros((), values.dtype))
    return jnp.sum(kept, axis=-1)


def segment_ids(positions, doc_lengths):
    offsets = running_sum(doc_lengths) - doc_lengths
    return jnp.sum((offsets[None, :] <= positions[:, None]).astype(jnp.int32), axis=1)


def start_flags(positions, doc_lengths):
    offsets = running_sum(doc_lengths) - doc_lengths
    return jnp.any(offsets[None, :] == positions[:, None], axis=1)


def causal_conv(values, margin, weights, positions, segment, doc_lengths):
    row_count = values.shape[0]
    tap_count = weights.shape[0]
    extended = jnp.concatenate([margin, values], axis=0).astype(jnp.float32)
    conv_sum = jnp.zeros(values.shape, jnp.float32)
    for tap_index in range(tap_count):
        source = positions - (tap_count - 1) + tap_index
        inside = (segment_ids(source, doc_lengths) == segment).astype(jnp.float32)
        conv_sum = (
            conv_sum
            + extended[tap_index : tap_index + row_count]
            * weights[tap_index].astype(jnp.float32)[None, :]
            * inside[:, None]
        )
    return jax.nn.silu(conv_sum)


def unit_heads(values, head_size):
    shaped = values.reshape(values.shape[0], -1, head_size)
    return shaped * lax.rsqrt(jnp.sum(shaped * shaped, axis=-1, keepdims=True) + 1e-06)


def compose(first_pair, second_pair):
    joined_map = jnp.einsum(
        "hij,hjk->hik", second_pair[0], first_pair[0], precision=EXACT_PRECISION
    )
    joined_shift = (
        jnp.einsum("hij,hjk->hik", second_pair[0], first_pair[1], precision=EXACT_PRECISION)
        + second_pair[1]
    )
    return (joined_map, joined_shift)


def unit_lower_inverse(lower_part, block_len):
    identity = jnp.eye(block_len, dtype=jnp.float32)
    power = -lower_part
    inverse = identity + power
    for _ in range(max(block_len - 1, 1).bit_length() - 1):
        power = jnp.einsum("nhij,nhjk->nhik", power, power, precision=EXACT_PRECISION)
        inverse = jnp.einsum(
            "nhij,nhjk->nhik", inverse, identity + power, precision=EXACT_PRECISION
        )
    return inverse


def delta_blocks(queries, keys_unit, values, beta_gate, log_rates, segment, starts):
    row_count, head_count, key_size = keys_unit.shape
    value_size = values.shape[2]
    block_len = BLOCK
    block_count = row_count // block_len

    def to_blocks(array):
        return jnp.swapaxes(array.reshape((block_count, block_len) + array.shape[1:]), 1, 2)

    query_blk = to_blocks(queries)
    key_blk = to_blocks(keys_unit)
    value_blk = to_blocks(values)
    beta_blk = to_blocks(beta_gate)
    cumulative = running_sum(to_blocks(log_rates))
    segment_blk = segment.reshape(block_count, block_len)
    fresh_count = running_sum(starts.reshape(block_count, block_len).astype(jnp.int32))
    later_row = lax.broadcasted_iota(jnp.int32, (block_len, block_len), 0)
    earlier_col = lax.broadcasted_iota(jnp.int32, (block_len, block_len), 1)
    visible = (later_row >= earlier_col)[None] & (
        segment_blk[:, :, None] == segment_blk[:, None, :]
    )
    visible = visible[:, None]
    spread = cumulative[..., :, None] - cumulative[..., None, :]
    decay_mat = jnp.where(visible, jnp.exp(jnp.where(visible, spread, 0.0)), 0.0)
    carried = jnp.where((fresh_count == 0)[:, None, :], jnp.exp(cumulative), 0.0)
    key_key = jnp.einsum("nhik,nhjk->nhij", key_blk, key_blk, precision=EXACT_PRECISION)
    strict = (later_row > earlier_col).astype(jnp.float32)
    lower_part = decay_mat * strict * key_key * beta_blk[..., None, :]
    inverse = unit_lower_inverse(lower_part, block_len)
    right_side = jnp.concatenate([value_blk, carried[..., None] * key_blk], axis=-1)
    solved = jnp.einsum("nhij,nhjc->nhic", inverse, right_side, precision=EXACT_PRECISION)
    moved_values = solved[..., :value_size]
    moved_keys = solved[..., value_size:]
    query_key = jnp.einsum("nhik,nhjk->nhij", query_blk, key_blk, precision=EXACT_PRECISION)
    attend = decay_mat * query_key * beta_blk[..., None, :]
    out_zero = jnp.einsum("nhij,nhjv->nhiv", attend, moved_values, precision=EXACT_PRECISION)
    reach_part = carried[..., None] * query_blk - jnp.einsum(
        "nhij,nhjk->nhik", attend, moved_keys, precision=EXACT_PRECISION
    )
    weighted = (beta_blk * decay_mat[..., block_len - 1, :])[..., None] * key_blk
    block_map = carried[..., block_len - 1][..., None, None] * jnp.eye(
        key_size, dtype=jnp.float32
    ) - jnp.einsum("nhjk,nhjl->nhkl", weighted, moved_keys, precision=EXACT_PRECISION)
    block_shift = jnp.einsum("nhjk,nhjv->nhkv", weighted, moved_values, precision=EXACT_PRECISION)

    def advance(prefix, current):
        return (compose(prefix, current), prefix)

    eye_heads = jnp.broadcast_to(
        jnp.eye(key_size, dtype=jnp.float32), (head_count, key_size, key_size)
    )
    zero_heads = jnp.zeros((head_count, key_size, value_size), jnp.float32)
    device_pair, prefixes = lax.scan(advance, (eye_heads, zero_heads), (block_map, block_shift))
    baseline_output = out_zero + jnp.einsum(
        "nhik,nhkv->nhiv", reach_part, prefixes[1], precision=EXACT_PRECISION
    )
    complete_reach = jnp.einsum(
        "nhik,nhkl->nhil", reach_part, prefixes[0], precision=EXACT_PRECISION
    )
    return (device_pair, baseline_output, complete_reach, eye_heads, zero_heads)


def shards(
    lin_q,
    lin_k,
    lin_v,
    conv_q,
    conv_k,
    conv_v,
    lin_z,
    beta_logit,
    log_decay,
    attn_query,
    attn_gate,
    attn_kv,
    doc_lengths,
):
    row_count = lin_q.shape[0]
    seq_index = lax.axis_index("seq")
    positions = seq_index * row_count + jnp.arange(row_count, dtype=jnp.int32)
    segment = segment_ids(positions, doc_lengths)
    starts = start_flags(positions, doc_lengths)
    rim_from = row_count - conv_q.shape[0] + 1
    rim_q, rim_k, rim_v = passed_along(
        (lin_q[rim_from:], lin_k[rim_from:], lin_v[rim_from:]), "seq", 1
    )
    queries = unit_heads(
        causal_conv(lin_q, rim_q, conv_q, positions, segment, doc_lengths), DK
    ) * DK ** (-0.5)
    keys_unit = unit_heads(causal_conv(lin_k, rim_k, conv_k, positions, segment, doc_lengths), DK)
    values = causal_conv(lin_v, rim_v, conv_v, positions, segment, doc_lengths).reshape(
        row_count, -1, DV
    )
    head_count = values.shape[1]
    queries = jnp.repeat(queries, VALUE_HEADS // QKH, axis=1)
    keys_unit = jnp.repeat(keys_unit, VALUE_HEADS // QKH, axis=1)
    beta_gate = jax.nn.sigmoid(beta_logit)
    device_pair, baseline_output, complete_reach, eye_heads, zero_heads = delta_blocks(
        queries, keys_unit, values, beta_gate, log_decay, segment, starts
    )
    arriving_input = prefix_2(
        (device_pair[0], device_pair[1]), "seq", compose, (eye_heads, zero_heads)
    )
    delta_output = baseline_output + jnp.einsum(
        "dpjt,ptw->dpjw", complete_reach, arriving_input[1], precision=EXACT_PRECISION
    )
    delta_output = jnp.swapaxes(delta_output, 1, 2).reshape(row_count, head_count, DV)
    inverse_rms = lax.rsqrt(jnp.mean(delta_output * delta_output, axis=-1, keepdims=True) + 1e-06)
    gate_z = jax.nn.silu(lin_z.astype(jnp.float32).reshape(row_count, head_count, DV))
    delta_out = (
        (delta_output * inverse_rms * gate_z)
        .astype(jnp.bfloat16)
        .reshape(row_count, head_count * DV)
    )
    aq_local = attn_query.shape[1] // AD
    query_heads = attn_query.reshape(row_count, aq_local, AD)
    kv_head = lax.axis_index("head") * aq_local // (AQ // KVH)
    own_pair = lax.dynamic_index_in_dim(attn_kv, kv_head, axis=2, keepdims=False)
    score_scale = AD ** (-0.5)

    def absorb(running, kv_piece, first_row):
        row_top, row_total, accum = running
        piece_rows = kv_piece.shape[0]
        key_pos = first_row + jnp.arange(piece_rows, dtype=jnp.int32)
        key_seg = segment_ids(key_pos, doc_lengths)
        allowed = (
            (key_pos[None, :] <= positions[:, None])
            & (key_seg[None, :] == segment[:, None])
            & (key_pos[None, :] >= 0)
        )
        scores = (
            jnp.einsum(
                "qhd,kd->hqk", query_heads, kv_piece[:, 0], preferred_element_type=jnp.float32
            )
            * score_scale
        )
        masked = jnp.where(allowed[None], scores, NEGATIVE)
        new_top = jnp.maximum(row_top, jnp.max(masked, axis=-1))
        weights_f = jnp.where(allowed[None], jnp.exp(masked - new_top[..., None]), 0.0)
        rescale = jnp.exp(row_top - new_top)
        row_total = row_total * rescale + jnp.sum(weights_f, axis=-1)
        accum = accum * rescale[..., None] + jnp.einsum(
            "hqk,kd->hqd",
            weights_f.astype(jnp.bfloat16),
            kv_piece[:, 1],
            preferred_element_type=jnp.float32,
        )
        return (new_top, row_total, accum)

    start_state = (
        jnp.full((aq_local, row_count), NEGATIVE, jnp.float32),
        jnp.zeros((aq_local, row_count), jnp.float32),
        jnp.zeros((aq_local, row_count, AD), jnp.float32),
    )
    running = absorb(start_state, own_pair, seq_index * row_count)

    def hop(hop_step, loop_state):
        loop_running, kv_piece = loop_state
        kv_piece = passed_along(kv_piece, "seq", 1)
        loop_running = absorb(loop_running, kv_piece, (seq_index - hop_step - 1) * row_count)
        return (loop_running, kv_piece)

    running, _ = lax.fori_loop(0, lax.axis_size("seq") // 4, hop, (running, own_pair))
    row_top, row_total, accum = running
    attended = jnp.swapaxes(accum / row_total[..., None], 0, 1).reshape(row_count, aq_local * AD)
    attn_out = (attended * jax.nn.sigmoid(attn_gate.astype(jnp.float32))).astype(jnp.bfloat16)
    return (delta_out, attn_out)


BF = jnp.bfloat16
F32 = jnp.float32
LANES = 128
LOG2E = 1.4426950408889634


def mm(a, b, transposed=False):
    contract = ((1,), (1,)) if transposed else ((1,), (0,))
    return lax.dot_general(a, b, (contract, ((), ())), preferred_element_type=F32)


def halves(x):
    high = x.astype(BF)
    return high, (x - high.astype(F32)).astype(BF)


def block_diagonal(wide):
    zero = jnp.zeros((wide.shape[0], LANES), wide.dtype)
    return jnp.concatenate(
        [
            jnp.concatenate([wide[:, :LANES], zero], axis=1),
            jnp.concatenate([zero, wide[:, LANES:]], axis=1),
        ],
        axis=0,
    )


def changed(x, size):
    if size % 16:
        return x
    starts = range(size, x.shape[0], 2 * size)
    return jnp.concatenate([x[at : at + size] for at in starts], axis=0)


def lessened(x, change, size):
    if size % 16:
        return x - change
    parts = []
    for at in range(0, x.shape[0], 2 * size):
        parts.append(x[at : at + size])
        parts.append(x[at + size : at + 2 * size] - change[at // 2 : at // 2 + size])
    return jnp.concatenate(parts, axis=0)


def twice(x):
    return jnp.concatenate([x, x], axis=1)


def half_sigmoid(x):
    return 0.5 + 0.5 * jnp.tanh(0.5 * x)


def fused_kernel(
    count,
    doc_hbm,
    kv_hbm,
    q_hbm,
    k_hbm,
    v_hbm,
    conv_q_hbm,
    conv_k_hbm,
    conv_v_hbm,
    z_hbm,
    beta_hbm,
    decay_hbm,
    aq_hbm,
    ag_hbm,
    delta_out,
    attn_out,
    doc_ref,
    kv_raw,
    lin_q,
    lin_k,
    lin_v,
    conv_q,
    conv_k,
    conv_v,
    lin_z,
    beta_logit,
    log_decay,
    attn_query,
    attn_gate,
    rim_q,
    rim_k,
    rim_v,
    kv_own,
    kv_before,
    state_out,
    state_in,
    spread,
    local_out,
    reach_out,
    gates,
    load_sem,
    send_sem,
    recv_sem,
):
    rows = lin_q.shape[0]
    heads = lin_v.shape[1] // DV
    pairs = range(lin_k.shape[1] // DK)
    docs = doc_ref.shape[0]
    rim = rim_q.shape[0]
    index = lax.axis_index("seq")
    head_index = lax.axis_index("head")
    lane_of_pair = lax.rem(head_index, 2)
    sibling = head_index + 1 - 2 * lane_of_pair
    aq_local = attn_query.shape[1] // AD
    kv_head = head_index * aq_local // (AQ // KVH)
    barrier = pltpu.get_barrier_semaphore()
    mesh_id = pl.DeviceIdType.MESH

    @pl.when(index > 0)
    def _():
        pl.semaphore_signal(
            barrier, inc=1, device_id={"seq": index - 1}, device_id_type=mesh_id
        )
        pl.semaphore_signal(
            barrier, inc=1, device_id={"head": sibling}, device_id_type=mesh_id
        )

    loads = {}

    def load(name, source, target):
        copy = pltpu.make_async_copy(source, target, load_sem.at[len(loads)])
        copy.start()
        loads[name] = copy

    load("doc", doc_hbm, doc_ref)
    load("decay", decay_hbm, log_decay)
    load("beta", beta_hbm, beta_logit)
    load("k", k_hbm, lin_k)
    load("conv_k", conv_k_hbm, conv_k)
    load("v", v_hbm, lin_v)
    load("conv_v", conv_v_hbm, conv_v)
    for side in range(2):
        for at in range(AD // LANES):
            load(
                ("kv", side, at),
                kv_hbm.at[:, side, :, pl.ds(at * LANES, LANES)],
                kv_raw.at[side * (AD // LANES) + at],
            )
    load("q", q_hbm, lin_q)
    load("conv_q", conv_q_hbm, conv_q)
    load("aq", aq_hbm, attn_query)
    load("ag", ag_hbm, attn_gate)
    load("z", z_hbm, lin_z)

    def remote(source, target, slot, where):
        return pltpu.make_async_remote_copy(
            src_ref=source,
            dst_ref=target,
            send_sem=send_sem.at[slot],
            recv_sem=recv_sem.at[slot],
            device_id=where,
            device_id_type=mesh_id,
        )

    ahead = {"seq": index + 1}
    tail = pl.ds(rows - rim, rim)
    rims = [
        remote(k_hbm.at[tail, :], rim_k, 0, ahead),
        remote(v_hbm.at[tail, :], rim_v, 1, ahead),
        remote(q_hbm.at[tail, :], rim_q, 2, ahead),
    ]
    kv_ahead = remote(kv_own.at[lane_of_pair], kv_before.at[lane_of_pair], 3, ahead)
    kv_across = remote(
        kv_before.at[lane_of_pair], kv_before.at[lane_of_pair], 4, {"head": sibling}
    )
    states = [
        remote(state_out.at[pl.ds(2 * p, 2)], state_in.at[pl.ds(2 * p, 2)], 5 + p, ahead)
        for p in pairs
    ]

    @pl.when(index == 0)
    def _():
        rim_q[...] = jnp.zeros_like(rim_q)
        rim_k[...] = jnp.zeros_like(rim_k)
        rim_v[...] = jnp.zeros_like(rim_v)
        kv_before[...] = jnp.zeros_like(kv_before)
        state_in[...] = jnp.zeros_like(state_in)

    def arrived(*copies):
        @pl.when(index > 0)
        def _():
            for copy in copies:
                copy.wait_recv()

    def loaded(*names):
        for name in names:
            loads[name].wait()

    @pl.when((index > 0) & (index < count - 1))
    def _():
        pl.semaphore_wait(barrier, 2)

    @pl.when((index == 0) | (index == count - 1))
    def _():
        pl.semaphore_wait(barrier, 1)

    @pl.when(index < count - 1)
    def _():
        for copy in rims[:2]:
            copy.start()

    loaded("doc")
    first = index * rows
    offset = -first
    offsets = [offset]
    for d in range(docs - 1):
        offset = offset + doc_ref[d]
        offsets.append(offset)

    def begins(position):
        begin = jnp.full(position.shape, offsets[0], jnp.int32)
        for offset in offsets[1:]:
            begin = jnp.where(position >= offset, offset, begin)
        return begin

    square = (rows, rows)
    row_id = lax.broadcasted_iota(jnp.int32, square, 0)
    col_id = lax.broadcasted_iota(jnp.int32, square, 1)
    row_begin = begins(row_id)
    inside = col_id >= row_begin
    strict = jnp.where((row_id > col_id) & inside, 1.0, 0.0)
    visible = (row_id >= col_id) & inside
    visible_before = col_id - rows >= row_begin
    same = [None] + [jnp.where(row_id - s >= row_begin, 1.0, 0.0) for s in (1, 2, 3)]
    short_id = lax.broadcasted_iota(jnp.int32, (heads, rows), 1)
    short_begin = begins(short_id)
    last_begin = begins(jnp.full((heads, rows), rows - 1, jnp.int32))

    loaded("decay", "beta")
    rates = log_decay[...]
    part_a = rates.astype(BF)
    rest = rates - part_a.astype(F32)
    part_b = rest.astype(BF)
    part_c = (rest - part_b.astype(F32)).astype(BF)
    upper = jnp.where(row_id <= col_id, 1.0, 0.0).astype(BF)
    summed = (mm(part_a, upper) + mm(part_b, upper) + mm(part_c, upper)) * LOG2E
    beta_log = -jnp.log2(1.0 + jnp.exp(-beta_logit[...]))
    from_row = summed - beta_log
    carried_row = jnp.where(short_begin < 0, jnp.exp2(summed), 0.0)
    closing_row = jnp.where(
        short_id >= last_begin,
        jnp.exp2(summed[:, rows - 1 : rows] - from_row),
        0.0,
    )
    columns = jnp.concatenate(
        [summed, carried_row, closing_row, jnp.zeros((rows - 3 * heads, rows), F32)], axis=0
    ).T
    carried = [columns[:, heads + h : heads + h + 1] for h in range(heads)]
    closing = [columns[:, 2 * heads + h : 2 * heads + h + 1] for h in range(heads)]

    def decays(h):
        return jnp.exp2(jnp.minimum(columns[:, h : h + 1] - from_row[h : h + 1, :], 0.0))

    def unit(x):
        return x * lax.rsqrt(jnp.sum(x * x, axis=1, keepdims=True) + 1e-06)

    def plain(x):
        return x

    def conv(values, rim_ref, taps, at, slot, finish):
        width = pl.ds(at * LANES, LANES)
        scale = taps[:, width].astype(F32) * 0.5
        weights = [scale[3:4]] + [scale[3 - s : 4 - s] * same[s] for s in (1, 2, 3)]

        def silu(own, begin, end):
            total = own * weights[0]
            for s in (1, 2, 3):
                total = total + spread[slot, 8 + begin - s : 8 + end - s, :] * (
                    weights[s][begin:end]
                )
            return finish(total + total * jnp.tanh(total))

        own = values[:, width].astype(F32)
        spread[slot, 8 : 8 + rows, :] = own
        later = silu(own[8:], 8, rows)
        yield
        spread[slot, 0:8, :] = rim_ref[:, width].astype(F32)[rim - 8 :]
        yield jnp.concatenate([silu(own[:8], 0, 8), later], axis=0)

    base = 8
    near = jnp.where(twice((row_id // base) == (col_id // base)), -1.0, 0.0).astype(BF)
    eye = jnp.where(twice(row_id == col_id), 1.0, 0.0).astype(BF)
    joints = []
    size = base
    while size < rows:
        joints.append(
            jnp.where(
                twice(
                    ((row_id // (2 * size)) == (col_id // (2 * size)))
                    & ((row_id // size) != (col_id // size))
                ),
                1.0,
                0.0,
            ).astype(BF)
        )
        size *= 2

    convs = {}

    def begin_conv(kind, values, rim_ref, taps, at, slot, finish):
        convs[kind, at] = conv(values, rim_ref, taps, at, slot, finish)
        next(convs[kind, at])


    keys, key_high, decay, corrector, values_of, moved = {}, {}, {}, {}, {}, {}

    def chain(p):
        keys[p] = next(convs["k", p])
        key_high[p] = keys[p].astype(BF)
        product = mm(key_high[p], key_high[p], transposed=True) * strict
        lower = jnp.concatenate(
            [decay[2 * p] * product, decay[2 * p + 1] * product], axis=1
        ).astype(BF)
        yield
        power = lower * near
        square_of = mm(power, block_diagonal(power)).astype(BF)
        key_turned = keys[p].T.astype(BF)
        yield
        both = mm(jnp.concatenate([square_of, power], axis=0), block_diagonal(square_of))
        whole = power.astype(F32) + square_of.astype(F32) + both[rows:]
        fourth = both[:rows].astype(BF)
        yield
        whole = whole + fourth.astype(F32) + mm(whole.astype(BF), block_diagonal(fourth))
        inverse = eye + whole.astype(BF)
        for stage, joint in enumerate(joints):
            yield
            if stage in VALUES_AT:
                h = 2 * p + VALUES_AT.index(stage)
                if h % 2 >= EARLY_V:
                    begin_conv("v", lin_v, rim_v, conv_v, h, len(pairs) + h, plain)
                values_of[h] = next(convs["v", h])
            size = base << stage
            middle = mm(changed(inverse, size), block_diagonal(lower * joint)).astype(BF)
            if stage + 1 < len(joints):
                yield
                inverse = lessened(
                    inverse, mm(middle, block_diagonal(inverse)).astype(BF), size
                )
        corrector[p] = (inverse - eye, middle)
        wide = jnp.concatenate([values_of[2 * p], values_of[2 * p + 1]], axis=1)
        part = wide + mm(corrector[p][0], block_diagonal(wide.astype(BF)))
        yield
        moved[p] = lessened(part, mm(middle, block_diagonal(part.astype(BF))), rows // 2)
        ending = jnp.concatenate(
            [
                closing[2 * p] * moved[p][:, :DV],
                closing[2 * p + 1] * moved[p][:, DV:],
            ],
            axis=1,
        ).astype(BF)
        yield
        made = mm(key_turned, ending).astype(BF)
        state_out[2 * p] = made[:, :DV]
        state_out[2 * p + 1] = made[:, DV:]

        @pl.when(index < count - 1)
        def _():
            states[p].start()

    def choose_kv():
        choice = jnp.where(
            lax.broadcasted_iota(jnp.int32, (rows, 2 * rows), 1)
            == 2 * lax.broadcasted_iota(jnp.int32, (rows, 2 * rows), 0) + kv_head,
            1.0,
            0.0,
        ).astype(BF)
        flat = kv_raw.reshape(2 * AD // LANES, 2 * rows, LANES)
        for side in range(2):
            parts = [flat[side * (AD // LANES) + at] for at in range(AD // LANES)]
            kv_own[side] = mm(choice, jnp.concatenate(parts, axis=1)).astype(BF)

        @pl.when(index < count - 1)
        def _():
            kv_ahead.start()
            rims[2].start()

    def local(p):
        if QUERY_LATE:
            begin_conv("q", lin_q, rim_q, conv_q, p, len(pairs) + heads + p, unit)
        query = next(convs["q", p]) * DK ** (-0.5)
        high, low = halves(query)
        key_low = (keys[p] - key_high[p].astype(F32)).astype(BF)
        product = mm(
            jnp.concatenate([high, low, high], axis=1),
            jnp.concatenate([key_high[p], key_high[p], key_low], axis=1),
            transposed=True,
        )
        product = jnp.where(visible, product, 0.0)
        yield
        wide = jnp.concatenate(
            [carried[2 * p] * keys[p], carried[2 * p + 1] * keys[p]], axis=1
        )
        part = wide + mm(corrector[p][0], block_diagonal(wide.astype(BF)))
        moved_keys = lessened(
            part, mm(corrector[p][1], block_diagonal(part.astype(BF))), rows // 2
        ).astype(BF)
        values_high, values_low = halves(moved[p])
        for half in range(2):
            yield
            h = 2 * p + half
            lanes = slice(half * LANES, (half + 1) * LANES)
            high, low = halves(decay[h] * product)
            right = jnp.concatenate([values_high[:, lanes], moved_keys[:, lanes]], axis=1)
            mixed = mm(
                jnp.concatenate([high, low], axis=1), jnp.concatenate([right, right], axis=0)
            )
            local_out[h] = mixed[:, :DV] + mm(high, values_low[:, lanes])
            reach_out[h] = (carried[h] * query - mixed[:, DV:]).astype(BF)

    def forward_kv():
        arrived(kv_ahead)

        @pl.when(index > 0)
        def _():
            kv_across.start()

    def attend(a):
        if a == 0:
            arrived(kv_across)
        allowed = jnp.concatenate([visible_before, visible], axis=1)
        all_keys = jnp.concatenate([kv_before[0], kv_own[0]], axis=0)
        width = pl.ds(a * AD, AD)
        scores = mm(attn_query[:, width], all_keys, transposed=True)
        masked = jnp.where(allowed, scores, NEGATIVE)
        top = jnp.max(masked, axis=1, keepdims=True)
        yield
        weights = jnp.exp2((masked - top) * (AD ** (-0.5) * LOG2E))
        total = jnp.sum(weights, axis=1, keepdims=True)
        gate = half_sigmoid(attn_gate[:, width].astype(F32)) * (1.0 / total)
        yield
        all_values = jnp.concatenate([kv_before[1], kv_own[1]], axis=0)
        attn_out[:, width] = (mm(weights.astype(BF), all_values) * gate).astype(BF)

    def gate_values(p):
        for h in (2 * p, 2 * p + 1):
            gate = lin_z[:, pl.ds(h * DV, DV)].astype(F32) * 0.5
            gates[h] = gate + gate * jnp.tanh(gate)

    loaded("k", "conv_k")
    for p in pairs:
        begin_conv("k", lin_k, rim_k, conv_k, p, p, unit)
    loaded("v", "conv_v")
    for h in range(heads):
        if h % 2 < EARLY_V:
            begin_conv("v", lin_v, rim_v, conv_v, h, len(pairs) + h, plain)
        decay[h] = decays(h)
    loaded(*[("kv", side, at) for side in range(2) for at in range(AD // LANES)])
    choose_kv()
    loaded("q", "conv_q", "aq", "ag", "z")
    for p in pairs:
        if not QUERY_LATE:
            begin_conv("q", lin_q, rim_q, conv_q, p, len(pairs) + heads + p, unit)
    for p in EARLY_GATES:
        gate_values(p)
    arrived(rims[0])
    chains = [chain(p) for p in pairs]
    locals_of = [local(p) for p in pairs]
    attends = [attend(a) for a in range(aq_local)]
    pieces = []
    for name in PIECES:
        kind, at = name[0], int(name[1])
        if kind == "q":
            pieces.append((0, functools.partial(next, locals_of[at], None)))
        elif kind == "m":
            pieces.append((STARTS[at] + 15, functools.partial(next, locals_of[at], None)))
        elif kind == "f":
            pieces.append((0, forward_kv))
        elif kind == "a":
            pieces.append((0, functools.partial(next, attends[at], None)))
        else:
            pieces.append((0, functools.partial(gate_values, at)))
    for step in range(max(STARTS) + 15):
        if step == TAIL_AT:
            arrived(rims[1])
        for p in pairs:
            if step >= STARTS[p]:
                next(chains[p], None)
        if step >= PIECES_FROM and (step - PIECES_FROM) % PIECES_EVERY == 0:
            ready = [item for item in pieces if item[0] <= step]
            if ready:
                pieces.remove(ready[0])
                ready[0][1]()
    arrived(rims[2])
    for _, piece in pieces:
        piece()

    for p in pairs:
        arrived(states[p])
        for h in (2 * p, 2 * p + 1):
            value = local_out[h] + mm(reach_out[h], state_in[h])
            scale = lax.rsqrt(jnp.mean(value * value, axis=1, keepdims=True) + 1e-06)
            delta_out[:, pl.ds(h * DV, DV)] = (value * scale * gates[h]).astype(BF)

    @pl.when(index < count - 1)
    def _():
        for copy in rims + [kv_ahead] + states:
            copy.wait_send()

    @pl.when(index > 0)
    def _():
        kv_across.wait_send()


PIECES = ("f0",) + tuple(
    kind + str(at) for kind in ("z", "q", "m", "m", "m", "a", "a", "a") for at in range(4)
)
KERNEL_BYTES = 62_000_000
QUERY_LATE = True
EARLY_GATES = ()
PIECES_FROM = 100
PIECES_EVERY = 1
STARTS = (0, 0, 0, 0)
VALUES_AT = (1, 2)
TAIL_AT = 6
EARLY_V = 1


def deliver_kernel(delta_ref, attn_ref, delta_out, attn_out, sem):
    copies = [
        pltpu.make_async_copy(attn_ref, attn_out, sem.at[0]),
        pltpu.make_async_copy(delta_ref, delta_out, sem.at[1]),
    ]
    for copy in copies:
        copy.start()
    for copy in copies:
        copy.wait()


def fused(
    lin_q,
    lin_k,
    lin_v,
    conv_q,
    conv_k,
    conv_v,
    lin_z,
    beta_logit,
    log_decay,
    attn_query,
    attn_gate,
    attn_kv,
    doc_lengths,
):
    rows = lin_q.shape[0]
    heads = lin_v.shape[1] // DV
    pair_count = lin_k.shape[1] // DK
    streamed = (
        lin_q,
        lin_k,
        lin_v,
        conv_q,
        conv_k,
        conv_v,
        lin_z,
        beta_logit.T,
        log_decay.T,
        attn_query,
        attn_gate,
    )
    vmem = pl.BlockSpec(memory_space=pltpu.VMEM)
    hbm = pl.BlockSpec(memory_space=pltpu.HBM)
    rim = 16
    outs = (
        jax.ShapeDtypeStruct(lin_z.shape, BF),
        jax.ShapeDtypeStruct(attn_query.shape, BF),
    )
    lane_parts = 2 * AD // LANES
    delta, attn = pl.pallas_call(
        functools.partial(fused_kernel, lax.axis_size("seq")),
        out_shape=(pltpu.VMEM(lin_z.shape, BF), pltpu.VMEM(attn_query.shape, BF)),
        in_specs=[hbm] * 13,
        out_specs=(vmem, vmem),
        scratch_shapes=[
            pltpu.SMEM(doc_lengths.shape, jnp.int32),
            pltpu.VMEM((lane_parts, rows, KVH, LANES), BF),
        ]
        + [pltpu.VMEM(x.shape, x.dtype) for x in streamed]
        + [
            pltpu.VMEM((rim, lin_q.shape[1]), BF),
            pltpu.VMEM((rim, lin_k.shape[1]), BF),
            pltpu.VMEM((rim, lin_v.shape[1]), BF),
            pltpu.VMEM((2, rows, AD), BF),
            pltpu.VMEM((2, rows, AD), BF),
            pltpu.VMEM((heads, DK, DV), BF),
            pltpu.VMEM((heads, DK, DV), BF),
            pltpu.VMEM((2 * pair_count + heads, rows + 8, LANES), F32),
            pltpu.VMEM((heads, rows, DV), F32),
            pltpu.VMEM((heads, rows, DK), BF),
            pltpu.VMEM((heads, rows, DV), F32),
            pltpu.SemaphoreType.DMA((12 + lane_parts,)),
            pltpu.SemaphoreType.DMA((5 + pair_count,)),
            pltpu.SemaphoreType.DMA((5 + pair_count,)),
        ],
        compiler_params=pltpu.CompilerParams(
            collective_id=0, has_side_effects=True, vmem_limit_bytes=KERNEL_BYTES
        ),
    )(doc_lengths, attn_kv, *streamed)
    return pl.pallas_call(
        deliver_kernel,
        out_shape=outs,
        in_specs=[vmem, vmem],
        out_specs=(hbm, hbm),
        scratch_shapes=[pltpu.SemaphoreType.DMA((2,))],
        compiler_params=pltpu.CompilerParams(vmem_limit_bytes=1 << 20),
    )(delta, attn)


def solution(mesh):
    near = mesh.shape["seq"] == 4
    return jax.shard_map(
        fused if near else shards,
        mesh=mesh,
        in_specs=(
            P(("grp", "seq"), "head"),
            P(("grp", "seq"), "head"),
            P(("grp", "seq"), "head"),
            P(None, "head"),
            P(None, "head"),
            P(None, "head"),
            P(("grp", "seq"), "head"),
            P(("grp", "seq"), "head"),
            P(("grp", "seq"), "head"),
            P(("grp", "seq"), "head"),
            P(("grp", "seq"), "head"),
            P(("grp", "seq"), None, None, None),
            P("grp"),
        ),
        out_specs=(P(("grp", "seq"), "head"), P(("grp", "seq"), "head")),
        check_vma=False,
    )
```

```python
import functools

import jax
import jax.numpy as jnp
from jax import lax
from jax.experimental import pallas as pl
from jax.experimental.pallas import tpu as pltpu
from jax.sharding import PartitionSpec as P

DK = 128
DV = 128
QKH = 16
VALUE_HEADS = 32
AQ = 16
KVH = 2
AD = 256
BLOCK = 64


EXACT_PRECISION = lax.Precision.HIGHEST
NEGATIVE = -1e30


def passed_along(value, axis, steps):
    count = lax.axis_size(axis)
    initial, last = (max(0, -steps), min(count, count - steps))
    return lax.ppermute(value, axis, [(source, source + steps) for source in range(initial, last)])


def prefix_2(value, axis, combine, identity):
    length, index = (lax.axis_size(axis), lax.axis_index(axis))
    everything = jax.tree.map(
        lambda part, kind: lax.all_gather(part.astype(kind), axis),
        value,
        (jnp.bfloat16, jnp.bfloat16),
    )
    start = jax.tree.map(
        lambda part, zero: jnp.broadcast_to(jnp.asarray(zero, part.dtype), part.shape),
        value,
        identity,
    )

    def step(k, before):
        reached = k < index
        new = combine(
            before, jax.tree.map(lambda part, own: part[k].astype(own.dtype), everything, value)
        )
        return jax.tree.map(lambda a, b: jnp.where(reached, a, b), new, before)

    return lax.fori_loop(0, length, step, start)


def running_sum(values):
    count = values.shape[-1]
    later = lax.broadcasted_iota(jnp.int32, (count, count), 0)
    earlier = lax.broadcasted_iota(jnp.int32, (count, count), 1)
    kept = jnp.where(later >= earlier, values[..., None, :], jnp.zeros((), values.dtype))
    return jnp.sum(kept, axis=-1)


def segment_ids(positions, doc_lengths):
    offsets = running_sum(doc_lengths) - doc_lengths
    return jnp.sum((offsets[None, :] <= positions[:, None]).astype(jnp.int32), axis=1)


def start_flags(positions, doc_lengths):
    offsets = running_sum(doc_lengths) - doc_lengths
    return jnp.any(offsets[None, :] == positions[:, None], axis=1)


def causal_conv(values, margin, weights, positions, segment, doc_lengths):
    row_count = values.shape[0]
    tap_count = weights.shape[0]
    extended = jnp.concatenate([margin, values], axis=0).astype(jnp.float32)
    conv_sum = jnp.zeros(values.shape, jnp.float32)
    for tap_index in range(tap_count):
        source = positions - (tap_count - 1) + tap_index
        inside = (segment_ids(source, doc_lengths) == segment).astype(jnp.float32)
        conv_sum = (
            conv_sum
            + extended[tap_index : tap_index + row_count]
            * weights[tap_index].astype(jnp.float32)[None, :]
            * inside[:, None]
        )
    return jax.nn.silu(conv_sum)


def unit_heads(values, head_size):
    shaped = values.reshape(values.shape[0], -1, head_size)
    return shaped * lax.rsqrt(jnp.sum(shaped * shaped, axis=-1, keepdims=True) + 1e-06)


def compose(first_pair, second_pair):
    joined_map = jnp.einsum(
        "hij,hjk->hik", second_pair[0], first_pair[0], precision=EXACT_PRECISION
    )
    joined_shift = (
        jnp.einsum("hij,hjk->hik", second_pair[0], first_pair[1], precision=EXACT_PRECISION)
        + second_pair[1]
    )
    return (joined_map, joined_shift)


def unit_lower_inverse(lower_part, block_len):
    identity = jnp.eye(block_len, dtype=jnp.float32)
    power = -lower_part
    inverse = identity + power
    for _ in range(max(block_len - 1, 1).bit_length() - 1):
        power = jnp.einsum("nhij,nhjk->nhik", power, power, precision=EXACT_PRECISION)
        inverse = jnp.einsum(
            "nhij,nhjk->nhik", inverse, identity + power, precision=EXACT_PRECISION
        )
    return inverse


def delta_blocks(queries, keys_unit, values, beta_gate, log_rates, segment, starts):
    row_count, head_count, key_size = keys_unit.shape
    value_size = values.shape[2]
    block_len = BLOCK
    block_count = row_count // block_len

    def to_blocks(array):
        return jnp.swapaxes(array.reshape((block_count, block_len) + array.shape[1:]), 1, 2)

    query_blk = to_blocks(queries)
    key_blk = to_blocks(keys_unit)
    value_blk = to_blocks(values)
    beta_blk = to_blocks(beta_gate)
    cumulative = running_sum(to_blocks(log_rates))
    segment_blk = segment.reshape(block_count, block_len)
    fresh_count = running_sum(starts.reshape(block_count, block_len).astype(jnp.int32))
    later_row = lax.broadcasted_iota(jnp.int32, (block_len, block_len), 0)
    earlier_col = lax.broadcasted_iota(jnp.int32, (block_len, block_len), 1)
    visible = (later_row >= earlier_col)[None] & (
        segment_blk[:, :, None] == segment_blk[:, None, :]
    )
    visible = visible[:, None]
    spread = cumulative[..., :, None] - cumulative[..., None, :]
    decay_mat = jnp.where(visible, jnp.exp(jnp.where(visible, spread, 0.0)), 0.0)
    carried = jnp.where((fresh_count == 0)[:, None, :], jnp.exp(cumulative), 0.0)
    key_key = jnp.einsum("nhik,nhjk->nhij", key_blk, key_blk, precision=EXACT_PRECISION)
    strict = (later_row > earlier_col).astype(jnp.float32)
    lower_part = decay_mat * strict * key_key * beta_blk[..., None, :]
    inverse = unit_lower_inverse(lower_part, block_len)
    right_side = jnp.concatenate([value_blk, carried[..., None] * key_blk], axis=-1)
    solved = jnp.einsum("nhij,nhjc->nhic", inverse, right_side, precision=EXACT_PRECISION)
    moved_values = solved[..., :value_size]
    moved_keys = solved[..., value_size:]
    query_key = jnp.einsum("nhik,nhjk->nhij", query_blk, key_blk, precision=EXACT_PRECISION)
    attend = decay_mat * query_key * beta_blk[..., None, :]
    out_zero = jnp.einsum("nhij,nhjv->nhiv", attend, moved_values, precision=EXACT_PRECISION)
    reach_part = carried[..., None] * query_blk - jnp.einsum(
        "nhij,nhjk->nhik", attend, moved_keys, precision=EXACT_PRECISION
    )
    weighted = (beta_blk * decay_mat[..., block_len - 1, :])[..., None] * key_blk
    block_map = carried[..., block_len - 1][..., None, None] * jnp.eye(
        key_size, dtype=jnp.float32
    ) - jnp.einsum("nhjk,nhjl->nhkl", weighted, moved_keys, precision=EXACT_PRECISION)
    block_shift = jnp.einsum("nhjk,nhjv->nhkv", weighted, moved_values, precision=EXACT_PRECISION)

    def advance(prefix, current):
        return (compose(prefix, current), prefix)

    eye_heads = jnp.broadcast_to(
        jnp.eye(key_size, dtype=jnp.float32), (head_count, key_size, key_size)
    )
    zero_heads = jnp.zeros((head_count, key_size, value_size), jnp.float32)
    device_pair, prefixes = lax.scan(advance, (eye_heads, zero_heads), (block_map, block_shift))
    baseline_output = out_zero + jnp.einsum(
        "nhik,nhkv->nhiv", reach_part, prefixes[1], precision=EXACT_PRECISION
    )
    complete_reach = jnp.einsum(
        "nhik,nhkl->nhil", reach_part, prefixes[0], precision=EXACT_PRECISION
    )
    return (device_pair, baseline_output, complete_reach, eye_heads, zero_heads)


def shards(
    lin_q,
    lin_k,
    lin_v,
    conv_q,
    conv_k,
    conv_v,
    lin_z,
    beta_logit,
    log_decay,
    attn_query,
    attn_gate,
    attn_kv,
    doc_lengths,
):
    row_count = lin_q.shape[0]
    seq_index = lax.axis_index("seq")
    positions = seq_index * row_count + jnp.arange(row_count, dtype=jnp.int32)
    segment = segment_ids(positions, doc_lengths)
    starts = start_flags(positions, doc_lengths)
    rim_from = row_count - conv_q.shape[0] + 1
    rim_q, rim_k, rim_v = passed_along(
        (lin_q[rim_from:], lin_k[rim_from:], lin_v[rim_from:]), "seq", 1
    )
    queries = unit_heads(
        causal_conv(lin_q, rim_q, conv_q, positions, segment, doc_lengths), DK
    ) * DK ** (-0.5)
    keys_unit = unit_heads(causal_conv(lin_k, rim_k, conv_k, positions, segment, doc_lengths), DK)
    values = causal_conv(lin_v, rim_v, conv_v, positions, segment, doc_lengths).reshape(
        row_count, -1, DV
    )
    head_count = values.shape[1]
    queries = jnp.repeat(queries, VALUE_HEADS // QKH, axis=1)
    keys_unit = jnp.repeat(keys_unit, VALUE_HEADS // QKH, axis=1)
    beta_gate = jax.nn.sigmoid(beta_logit)
    device_pair, baseline_output, complete_reach, eye_heads, zero_heads = delta_blocks(
        queries, keys_unit, values, beta_gate, log_decay, segment, starts
    )
    arriving_input = prefix_2(
        (device_pair[0], device_pair[1]), "seq", compose, (eye_heads, zero_heads)
    )
    delta_output = baseline_output + jnp.einsum(
        "dpjt,ptw->dpjw", complete_reach, arriving_input[1], precision=EXACT_PRECISION
    )
    delta_output = jnp.swapaxes(delta_output, 1, 2).reshape(row_count, head_count, DV)
    inverse_rms = lax.rsqrt(jnp.mean(delta_output * delta_output, axis=-1, keepdims=True) + 1e-06)
    gate_z = jax.nn.silu(lin_z.astype(jnp.float32).reshape(row_count, head_count, DV))
    delta_out = (
        (delta_output * inverse_rms * gate_z)
        .astype(jnp.bfloat16)
        .reshape(row_count, head_count * DV)
    )
    aq_local = attn_query.shape[1] // AD
    query_heads = attn_query.reshape(row_count, aq_local, AD)
    kv_head = lax.axis_index("head") * aq_local // (AQ // KVH)
    own_pair = lax.dynamic_index_in_dim(attn_kv, kv_head, axis=2, keepdims=False)
    score_scale = AD ** (-0.5)

    def absorb(running, kv_piece, first_row):
        row_top, row_total, accum = running
        piece_rows = kv_piece.shape[0]
        key_pos = first_row + jnp.arange(piece_rows, dtype=jnp.int32)
        key_seg = segment_ids(key_pos, doc_lengths)
        allowed = (
            (key_pos[None, :] <= positions[:, None])
            & (key_seg[None, :] == segment[:, None])
            & (key_pos[None, :] >= 0)
        )
        scores = (
            jnp.einsum(
                "qhd,kd->hqk", query_heads, kv_piece[:, 0], preferred_element_type=jnp.float32
            )
            * score_scale
        )
        masked = jnp.where(allowed[None], scores, NEGATIVE)
        new_top = jnp.maximum(row_top, jnp.max(masked, axis=-1))
        weights_f = jnp.where(allowed[None], jnp.exp(masked - new_top[..., None]), 0.0)
        rescale = jnp.exp(row_top - new_top)
        row_total = row_total * rescale + jnp.sum(weights_f, axis=-1)
        accum = accum * rescale[..., None] + jnp.einsum(
            "hqk,kd->hqd",
            weights_f.astype(jnp.bfloat16),
            kv_piece[:, 1],
            preferred_element_type=jnp.float32,
        )
        return (new_top, row_total, accum)

    start_state = (
        jnp.full((aq_local, row_count), NEGATIVE, jnp.float32),
        jnp.zeros((aq_local, row_count), jnp.float32),
        jnp.zeros((aq_local, row_count, AD), jnp.float32),
    )
    running = absorb(start_state, own_pair, seq_index * row_count)

    def hop(hop_step, loop_state):
        loop_running, kv_piece = loop_state
        kv_piece = passed_along(kv_piece, "seq", 1)
        loop_running = absorb(loop_running, kv_piece, (seq_index - hop_step - 1) * row_count)
        return (loop_running, kv_piece)

    running, _ = lax.fori_loop(0, lax.axis_size("seq") // 4, hop, (running, own_pair))
    row_top, row_total, accum = running
    attended = jnp.swapaxes(accum / row_total[..., None], 0, 1).reshape(row_count, aq_local * AD)
    attn_out = (attended * jax.nn.sigmoid(attn_gate.astype(jnp.float32))).astype(jnp.bfloat16)
    return (delta_out, attn_out)


BF = jnp.bfloat16
F32 = jnp.float32
LANES = 128
LOG2E = 1.4426950408889634


def mm(a, b, transposed=False):
    contract = ((1,), (1,)) if transposed else ((1,), (0,))
    return lax.dot_general(a, b, (contract, ((), ())), preferred_element_type=F32)


def halves(x):
    high = x.astype(BF)
    return high, (x - high.astype(F32)).astype(BF)


def block_diagonal(wide):
    zero = jnp.zeros((wide.shape[0], LANES), wide.dtype)
    return jnp.concatenate(
        [
            jnp.concatenate([wide[:, :LANES], zero], axis=1),
            jnp.concatenate([zero, wide[:, LANES:]], axis=1),
        ],
        axis=0,
    )


def twice(x):
    return jnp.concatenate([x, x], axis=1)


def half_sigmoid(x):
    return 0.5 + 0.5 * jnp.tanh(0.5 * x)


def fused_kernel(
    count,
    doc_hbm,
    kv_hbm,
    q_hbm,
    k_hbm,
    v_hbm,
    conv_q_hbm,
    conv_k_hbm,
    conv_v_hbm,
    z_hbm,
    beta_hbm,
    decay_hbm,
    aq_hbm,
    ag_hbm,
    delta_out,
    attn_out,
    doc_ref,
    kv_raw,
    lin_q,
    lin_k,
    lin_v,
    conv_q,
    conv_k,
    conv_v,
    lin_z,
    beta_logit,
    log_decay,
    attn_query,
    attn_gate,
    rim_q,
    rim_k,
    rim_v,
    kv_own,
    kv_before,
    state_out,
    state_in,
    spread,
    local_out,
    reach_out,
    gates,
    load_sem,
    send_sem,
    recv_sem,
):
    rows = lin_q.shape[0]
    heads = lin_v.shape[1] // DV
    pairs = range(lin_k.shape[1] // DK)
    docs = doc_ref.shape[0]
    rim = rim_q.shape[0]
    index = lax.axis_index("seq")
    head_index = lax.axis_index("head")
    lane_of_pair = lax.rem(head_index, 2)
    sibling = head_index + 1 - 2 * lane_of_pair
    aq_local = attn_query.shape[1] // AD
    kv_head = head_index * aq_local // (AQ // KVH)
    barrier = pltpu.get_barrier_semaphore()
    mesh_id = pl.DeviceIdType.MESH

    @pl.when(index > 0)
    def _():
        pl.semaphore_signal(
            barrier, inc=1, device_id={"seq": index - 1}, device_id_type=mesh_id
        )
        pl.semaphore_signal(
            barrier, inc=1, device_id={"head": sibling}, device_id_type=mesh_id
        )

    loads = {}

    def load(name, source, target):
        copy = pltpu.make_async_copy(source, target, load_sem.at[len(loads)])
        copy.start()
        loads[name] = copy

    load("doc", doc_hbm, doc_ref)
    load("decay", decay_hbm, log_decay)
    load("beta", beta_hbm, beta_logit)
    load("k", k_hbm, lin_k)
    load("conv_k", conv_k_hbm, conv_k)
    load("v", v_hbm, lin_v)
    load("conv_v", conv_v_hbm, conv_v)
    for side in range(2):
        for at in range(AD // LANES):
            load(
                ("kv", side, at),
                kv_hbm.at[:, side, :, pl.ds(at * LANES, LANES)],
                kv_raw.at[side * (AD // LANES) + at],
            )
    load("q", q_hbm, lin_q)
    load("conv_q", conv_q_hbm, conv_q)
    load("aq", aq_hbm, attn_query)
    load("ag", ag_hbm, attn_gate)
    load("z", z_hbm, lin_z)

    def remote(source, target, slot, where):
        return pltpu.make_async_remote_copy(
            src_ref=source,
            dst_ref=target,
            send_sem=send_sem.at[slot],
            recv_sem=recv_sem.at[slot],
            device_id=where,
            device_id_type=mesh_id,
        )

    ahead = {"seq": index + 1}
    tail = pl.ds(rows - rim, rim)
    rims = [
        remote(k_hbm.at[tail, :], rim_k, 0, ahead),
        remote(v_hbm.at[tail, :], rim_v, 1, ahead),
        remote(q_hbm.at[tail, :], rim_q, 2, ahead),
    ]
    kv_ahead = remote(kv_own.at[lane_of_pair], kv_before.at[lane_of_pair], 3, ahead)
    kv_across = remote(
        kv_before.at[lane_of_pair], kv_before.at[lane_of_pair], 4, {"head": sibling}
    )
    states = [
        remote(state_out.at[pl.ds(2 * p, 2)], state_in.at[pl.ds(2 * p, 2)], 5 + p, ahead)
        for p in pairs
    ]

    @pl.when(index == 0)
    def _():
        rim_q[...] = jnp.zeros_like(rim_q)
        rim_k[...] = jnp.zeros_like(rim_k)
        rim_v[...] = jnp.zeros_like(rim_v)
        kv_before[...] = jnp.zeros_like(kv_before)
        state_in[...] = jnp.zeros_like(state_in)

    def arrived(*copies):
        @pl.when(index > 0)
        def _():
            for copy in copies:
                copy.wait_recv()

    def loaded(*names):
        for name in names:
            loads[name].wait()

    @pl.when((index > 0) & (index < count - 1))
    def _():
        pl.semaphore_wait(barrier, 2)

    @pl.when((index == 0) | (index == count - 1))
    def _():
        pl.semaphore_wait(barrier, 1)

    @pl.when(index < count - 1)
    def _():
        for copy in rims[:2]:
            copy.start()

    loaded("doc")
    first = index * rows
    offset = -first
    offsets = [offset]
    for d in range(docs - 1):
        offset = offset + doc_ref[d]
        offsets.append(offset)

    def begins(position):
        begin = jnp.full(position.shape, offsets[0], jnp.int32)
        for offset in offsets[1:]:
            begin = jnp.where(position >= offset, offset, begin)
        return begin

    square = (rows, rows)
    row_id = lax.broadcasted_iota(jnp.int32, square, 0)
    col_id = lax.broadcasted_iota(jnp.int32, square, 1)
    row_begin = begins(row_id)
    inside = col_id >= row_begin
    strict = jnp.where((row_id > col_id) & inside, 1.0, 0.0)
    visible = (row_id >= col_id) & inside
    visible_before = col_id - rows >= row_begin
    same = [None] + [jnp.where(row_id - s >= row_begin, 1.0, 0.0) for s in (1, 2, 3)]
    short_id = lax.broadcasted_iota(jnp.int32, (heads, rows), 1)
    short_begin = begins(short_id)
    last_begin = begins(jnp.full((heads, rows), rows - 1, jnp.int32))

    loaded("decay", "beta")
    rates = log_decay[...]
    part_a = rates.astype(BF)
    rest = rates - part_a.astype(F32)
    part_b = rest.astype(BF)
    part_c = (rest - part_b.astype(F32)).astype(BF)
    upper = jnp.where(row_id <= col_id, 1.0, 0.0).astype(BF)
    summed = (mm(part_a, upper) + mm(part_b, upper) + mm(part_c, upper)) * LOG2E
    beta_log = -jnp.log2(1.0 + jnp.exp(-beta_logit[...]))
    from_row = summed - beta_log
    carried_row = jnp.where(short_begin < 0, jnp.exp2(summed), 0.0)
    closing_row = jnp.where(
        short_id >= last_begin,
        jnp.exp2(summed[:, rows - 1 : rows] - from_row),
        0.0,
    )
    columns = jnp.concatenate(
        [summed, carried_row, closing_row, jnp.zeros((rows - 3 * heads, rows), F32)], axis=0
    ).T
    carried = [columns[:, heads + h : heads + h + 1] for h in range(heads)]
    closing = [columns[:, 2 * heads + h : 2 * heads + h + 1] for h in range(heads)]

    def decays(h):
        return jnp.exp2(jnp.minimum(columns[:, h : h + 1] - from_row[h : h + 1, :], 0.0))

    def unit(x):
        return x * lax.rsqrt(jnp.sum(x * x, axis=1, keepdims=True) + 1e-06)

    def plain(x):
        return x

    def conv(values, rim_ref, taps, at, slot, finish):
        width = pl.ds(at * LANES, LANES)
        scale = taps[:, width].astype(F32) * 0.5
        weights = [scale[3:4]] + [scale[3 - s : 4 - s] * same[s] for s in (1, 2, 3)]

        def silu(own, begin, end):
            total = own * weights[0]
            for s in (1, 2, 3):
                total = total + spread[slot, 8 + begin - s : 8 + end - s, :] * (
                    weights[s][begin:end]
                )
            return finish(total + total * jnp.tanh(total))

        own = values[:, width].astype(F32)
        spread[slot, 8 : 8 + rows, :] = own
        later = silu(own[8:], 8, rows)
        yield
        spread[slot, 0:8, :] = rim_ref[:, width].astype(F32)[rim - 8 :]
        yield jnp.concatenate([silu(own[:8], 0, 8), later], axis=0)

    base = 8
    near = jnp.where(twice((row_id // base) == (col_id // base)), -1.0, 0.0).astype(BF)
    eye = jnp.where(twice(row_id == col_id), 1.0, 0.0).astype(BF)
    joints = []
    size = base
    while size < rows:
        joints.append(
            jnp.where(
                twice(
                    ((row_id // (2 * size)) == (col_id // (2 * size)))
                    & ((row_id // size) != (col_id // size))
                ),
                1.0,
                0.0,
            ).astype(BF)
        )
        size *= 2

    convs = {}

    def begin_conv(kind, values, rim_ref, taps, at, slot, finish):
        convs[kind, at] = conv(values, rim_ref, taps, at, slot, finish)
        next(convs[kind, at])


    keys, key_high, decay, corrector, values_of, moved = {}, {}, {}, {}, {}, {}

    def chain(p):
        keys[p] = next(convs["k", p])
        key_high[p] = keys[p].astype(BF)
        product = mm(key_high[p], key_high[p], transposed=True) * strict
        lower = jnp.concatenate(
            [decay[2 * p] * product, decay[2 * p + 1] * product], axis=1
        ).astype(BF)
        yield
        power = lower * near
        square_of = mm(power, block_diagonal(power)).astype(BF)
        key_turned = keys[p].T.astype(BF)
        yield
        both = mm(jnp.concatenate([square_of, power], axis=0), block_diagonal(square_of))
        whole = power.astype(F32) + square_of.astype(F32) + both[rows:]
        fourth = both[:rows].astype(BF)
        yield
        whole = whole + fourth.astype(F32) + mm(whole.astype(BF), block_diagonal(fourth))
        inverse = eye + whole.astype(BF)
        for stage, joint in enumerate(joints):
            yield
            if stage in VALUES_AT:
                h = 2 * p + VALUES_AT.index(stage)
                if h % 2 >= EARLY_V:
                    begin_conv("v", lin_v, rim_v, conv_v, h, len(pairs) + h, plain)
                values_of[h] = next(convs["v", h])
            middle = mm(inverse, block_diagonal(lower * joint)).astype(BF)
            if stage + 1 < len(joints):
                yield
                inverse = inverse - mm(middle, block_diagonal(inverse)).astype(BF)
        corrector[p] = (inverse - eye, middle)
        wide = jnp.concatenate([values_of[2 * p], values_of[2 * p + 1]], axis=1)
        part = wide + mm(corrector[p][0], block_diagonal(wide.astype(BF)))
        yield
        moved[p] = part - mm(middle, block_diagonal(part.astype(BF)))
        ending = jnp.concatenate(
            [
                closing[2 * p] * moved[p][:, :DV],
                closing[2 * p + 1] * moved[p][:, DV:],
            ],
            axis=1,
        ).astype(BF)
        yield
        made = mm(key_turned, ending).astype(BF)
        state_out[2 * p] = made[:, :DV]
        state_out[2 * p + 1] = made[:, DV:]

        @pl.when(index < count - 1)
        def _():
            states[p].start()

    def choose_kv():
        choice = jnp.where(
            lax.broadcasted_iota(jnp.int32, (rows, 2 * rows), 1)
            == 2 * lax.broadcasted_iota(jnp.int32, (rows, 2 * rows), 0) + kv_head,
            1.0,
            0.0,
        ).astype(BF)
        flat = kv_raw.reshape(2 * AD // LANES, 2 * rows, LANES)
        for side in range(2):
            parts = [flat[side * (AD // LANES) + at] for at in range(AD // LANES)]
            kv_own[side] = mm(choice, jnp.concatenate(parts, axis=1)).astype(BF)

        @pl.when(index < count - 1)
        def _():
            kv_ahead.start()
            rims[2].start()

    def local(p):
        if QUERY_LATE:
            begin_conv("q", lin_q, rim_q, conv_q, p, len(pairs) + heads + p, unit)
        query = next(convs["q", p]) * DK ** (-0.5)
        high, low = halves(query)
        key_low = (keys[p] - key_high[p].astype(F32)).astype(BF)
        product = mm(
            jnp.concatenate([high, low, high], axis=1),
            jnp.concatenate([key_high[p], key_high[p], key_low], axis=1),
            transposed=True,
        )
        product = jnp.where(visible, product, 0.0)
        yield
        wide = jnp.concatenate(
            [carried[2 * p] * keys[p], carried[2 * p + 1] * keys[p]], axis=1
        )
        part = wide + mm(corrector[p][0], block_diagonal(wide.astype(BF)))
        moved_keys = (part - mm(corrector[p][1], block_diagonal(part.astype(BF)))).astype(BF)
        values_high, values_low = halves(moved[p])
        for half in range(2):
            yield
            h = 2 * p + half
            lanes = slice(half * LANES, (half + 1) * LANES)
            high, low = halves(decay[h] * product)
            right = jnp.concatenate([values_high[:, lanes], moved_keys[:, lanes]], axis=1)
            mixed = mm(
                jnp.concatenate([high, low], axis=1), jnp.concatenate([right, right], axis=0)
            )
            local_out[h] = mixed[:, :DV] + mm(high, values_low[:, lanes])
            reach_out[h] = (carried[h] * query - mixed[:, DV:]).astype(BF)

    def forward_kv():
        arrived(kv_ahead)

        @pl.when(index > 0)
        def _():
            kv_across.start()

    def attend(a):
        if a == 0:
            arrived(kv_across)
        allowed = jnp.concatenate([visible_before, visible], axis=1)
        all_keys = jnp.concatenate([kv_before[0], kv_own[0]], axis=0)
        width = pl.ds(a * AD, AD)
        scores = mm(attn_query[:, width], all_keys, transposed=True)
        masked = jnp.where(allowed, scores, NEGATIVE)
        top = jnp.max(masked, axis=1, keepdims=True)
        yield
        weights = jnp.exp2((masked - top) * (AD ** (-0.5) * LOG2E))
        total = jnp.sum(weights, axis=1, keepdims=True)
        gate = half_sigmoid(attn_gate[:, width].astype(F32)) * (1.0 / total)
        yield
        all_values = jnp.concatenate([kv_before[1], kv_own[1]], axis=0)
        attn_out[:, width] = (mm(weights.astype(BF), all_values) * gate).astype(BF)

    def gate_values(p):
        for h in (2 * p, 2 * p + 1):
            gate = lin_z[:, pl.ds(h * DV, DV)].astype(F32) * 0.5
            gates[h] = gate + gate * jnp.tanh(gate)

    loaded("k", "conv_k")
    for p in pairs:
        begin_conv("k", lin_k, rim_k, conv_k, p, p, unit)
    loaded(*[("kv", side, at) for side in range(2) for at in range(AD // LANES)])
    choose_kv()
    loaded("v", "conv_v")
    for h in range(heads):
        if h % 2 < EARLY_V:
            begin_conv("v", lin_v, rim_v, conv_v, h, len(pairs) + h, plain)
        decay[h] = decays(h)
    loaded("q", "conv_q", "aq", "ag", "z")
    for p in pairs:
        if not QUERY_LATE:
            begin_conv("q", lin_q, rim_q, conv_q, p, len(pairs) + heads + p, unit)
    for p in EARLY_GATES:
        gate_values(p)
    arrived(rims[0])
    chains = [chain(p) for p in pairs]
    locals_of = [local(p) for p in pairs]
    attends = [attend(a) for a in range(aq_local)]
    pieces = []
    for name in PIECES:
        kind, at = name[0], int(name[1])
        if kind == "q":
            pieces.append((0, functools.partial(next, locals_of[at], None)))
        elif kind == "m":
            pieces.append((STARTS[at] + 15, functools.partial(next, locals_of[at], None)))
        elif kind == "f":
            pieces.append((0, forward_kv))
        elif kind == "a":
            pieces.append((0, functools.partial(next, attends[at], None)))
        else:
            pieces.append((0, functools.partial(gate_values, at)))
    for step in range(max(STARTS) + 15):
        if step == TAIL_AT:
            arrived(rims[1])
        for p in pairs:
            if step >= STARTS[p]:
                next(chains[p], None)
        if step >= PIECES_FROM and (step - PIECES_FROM) % PIECES_EVERY == 0:
            ready = [item for item in pieces if item[0] <= step]
            if ready:
                pieces.remove(ready[0])
                ready[0][1]()
    arrived(rims[2])
    for _, piece in pieces:
        piece()

    for p in pairs:
        arrived(states[p])
        for h in (2 * p, 2 * p + 1):
            value = local_out[h] + mm(reach_out[h], state_in[h])
            scale = lax.rsqrt(jnp.mean(value * value, axis=1, keepdims=True) + 1e-06)
            delta_out[:, pl.ds(h * DV, DV)] = (value * scale * gates[h]).astype(BF)

    @pl.when(index < count - 1)
    def _():
        for copy in rims + [kv_ahead] + states:
            copy.wait_send()

    @pl.when(index > 0)
    def _():
        kv_across.wait_send()


PIECES = ("f0",) + tuple(
    kind + str(at) for kind in ("z", "q", "m", "m", "m", "a", "a", "a") for at in range(4)
)
KERNEL_BYTES = 62_000_000
QUERY_LATE = True
EARLY_GATES = ()
PIECES_FROM = 100
PIECES_EVERY = 1
STARTS = (0, 0, 0, 0)
VALUES_AT = (1, 2)
TAIL_AT = 6
EARLY_V = 1


def deliver_kernel(delta_ref, attn_ref, delta_out, attn_out, sem):
    copies = [
        pltpu.make_async_copy(attn_ref, attn_out, sem.at[0]),
        pltpu.make_async_copy(delta_ref, delta_out, sem.at[1]),
    ]
    for copy in copies:
        copy.start()
    for copy in copies:
        copy.wait()


def fused(
    lin_q,
    lin_k,
    lin_v,
    conv_q,
    conv_k,
    conv_v,
    lin_z,
    beta_logit,
    log_decay,
    attn_query,
    attn_gate,
    attn_kv,
    doc_lengths,
):
    rows = lin_q.shape[0]
    heads = lin_v.shape[1] // DV
    pair_count = lin_k.shape[1] // DK
    streamed = (
        lin_q,
        lin_k,
        lin_v,
        conv_q,
        conv_k,
        conv_v,
        lin_z,
        beta_logit.T,
        log_decay.T,
        attn_query,
        attn_gate,
    )
    vmem = pl.BlockSpec(memory_space=pltpu.VMEM)
    hbm = pl.BlockSpec(memory_space=pltpu.HBM)
    rim = 16
    outs = (
        jax.ShapeDtypeStruct(lin_z.shape, BF),
        jax.ShapeDtypeStruct(attn_query.shape, BF),
    )
    lane_parts = 2 * AD // LANES
    delta, attn = pl.pallas_call(
        functools.partial(fused_kernel, lax.axis_size("seq")),
        out_shape=(pltpu.VMEM(lin_z.shape, BF), pltpu.VMEM(attn_query.shape, BF)),
        in_specs=[hbm] * 13,
        out_specs=(vmem, vmem),
        scratch_shapes=[
            pltpu.SMEM(doc_lengths.shape, jnp.int32),
            pltpu.VMEM((lane_parts, rows, KVH, LANES), BF),
        ]
        + [pltpu.VMEM(x.shape, x.dtype) for x in streamed]
        + [
            pltpu.VMEM((rim, lin_q.shape[1]), BF),
            pltpu.VMEM((rim, lin_k.shape[1]), BF),
            pltpu.VMEM((rim, lin_v.shape[1]), BF),
            pltpu.VMEM((2, rows, AD), BF),
            pltpu.VMEM((2, rows, AD), BF),
            pltpu.VMEM((heads, DK, DV), BF),
            pltpu.VMEM((heads, DK, DV), BF),
            pltpu.VMEM((2 * pair_count + heads, rows + 8, LANES), F32),
            pltpu.VMEM((heads, rows, DV), F32),
            pltpu.VMEM((heads, rows, DK), BF),
            pltpu.VMEM((heads, rows, DV), F32),
            pltpu.SemaphoreType.DMA((12 + lane_parts,)),
            pltpu.SemaphoreType.DMA((5 + pair_count,)),
            pltpu.SemaphoreType.DMA((5 + pair_count,)),
        ],
        compiler_params=pltpu.CompilerParams(
            collective_id=0, has_side_effects=True, vmem_limit_bytes=KERNEL_BYTES
        ),
    )(doc_lengths, attn_kv, *streamed)
    return pl.pallas_call(
        deliver_kernel,
        out_shape=outs,
        in_specs=[vmem, vmem],
        out_specs=(hbm, hbm),
        scratch_shapes=[pltpu.SemaphoreType.DMA((2,))],
        compiler_params=pltpu.CompilerParams(vmem_limit_bytes=1 << 20),
    )(delta, attn)


def solution(mesh):
    near = mesh.shape["seq"] == 4
    return jax.shard_map(
        fused if near else shards,
        mesh=mesh,
        in_specs=(
            P(("grp", "seq"), "head"),
            P(("grp", "seq"), "head"),
            P(("grp", "seq"), "head"),
            P(None, "head"),
            P(None, "head"),
            P(None, "head"),
            P(("grp", "seq"), "head"),
            P(("grp", "seq"), "head"),
            P(("grp", "seq"), "head"),
            P(("grp", "seq"), "head"),
            P(("grp", "seq"), "head"),
            P(("grp", "seq"), None, None, None),
            P("grp"),
        ),
        out_specs=(P(("grp", "seq"), "head"), P(("grp", "seq"), "head")),
        check_vma=False,
    )
```
